768 devices in a mesh: ta: 12 (over z_hi, x), gz: 16 (over y, core), gy: 4 (over z_lo).
Axes of the slice: x: 4, y: 8, z: 12 (z_hi: 3, z_lo: 4; z = z_hi * 4 + z_lo), core: 2. Of those that a mesh axis runs over, the one named last changes fastest.
Arguments:
- source: float32 [4, 3, 2, 24, 16, 1024], P(None, None, None, 'ta', 'gz', 'gy'), may hold values from -6 to 6
- link_rows: float32 [4, 2, 3, 2, 24, 16, 1024], P(None, None, None, None, 'ta', 'gz', 'gy'), may hold values from -1 to 1, as said below
- clover_diag: float32 [2, 6, 24, 16, 1024], P(None, None, 'ta', 'gz', 'gy'), may hold values from 0.6 to 1.4
- clover_off: float32 [2, 15, 2, 24, 16, 1024], P(None, None, None, 'ta', 'gz', 'gy'), may hold values from -0.72 to 0.72
Outputs:
- solution: float32 [4, 3, 2, 24, 16, 1024], P(None, None, None, 'ta', 'gz', 'gy')
- residual: float32 [4, 3, 2, 24, 16, 1024], P(None, None, None, 'ta', 'gz', 'gy')
The draws below stay inside these ranges and needn't reach their ends.
Inputs may be any that keep to these rules, and one draw needn't show every extreme that they name: `link_rows`: at every site and direction the two rows are the first two rows of a special unitary 3 x 3 matrix (real and imaginary parts along the fourth dimension).
All inputs are finite; a program needn't handle non-finite values.
Results may differ from the reference program's by a relative error of at most 0.000025.
Values sent between devices are 32-bit elements; how exact they have to be, the bound alone decides.
A program may use at most 32 MiB of HBM per device.

```python
import math
import jax
import jax.numpy as jnp
from jax import lax

NX = 32
ITERS = 4
NT = 24
NZ = 16
NY = 32
NYX = 1024


def pair_rotation(first_index, second_index, theta, alpha, beta):
    zero_field = jnp.zeros_like(theta)
    unit_field = jnp.ones_like(theta)
    matrix = [[(unit_field if row_index == col_index else zero_field, zero_field) for col_index in range(3)] for row_index in range(3)]
    cos_part = jnp.cos(theta)
    sin_part = jnp.sin(theta)
    diag_real = cos_part * jnp.cos(alpha)
    diag_imag = cos_part * jnp.sin(alpha)
    side_real = sin_part * jnp.cos(beta)
    side_imag = sin_part * jnp.sin(beta)
    matrix[first_index][first_index] = (diag_real, diag_imag)
    matrix[first_index][second_index] = (side_real, side_imag)
    matrix[second_index][first_index] = (-side_real, side_imag)
    matrix[second_index][second_index] = (diag_real, -diag_imag)
    return matrix


def complex_product(left, right):
    result = []
    for row_index in range(3):
        row_out = []
        for col_index in range(3):
            sum_real = 0.0
            sum_imag = 0.0
            for inner in range(3):
                left_real, left_imag = left[row_index][inner]
                right_real, right_imag = right[inner][col_index]
                sum_real = sum_real + left_real * right_real - left_imag * right_imag
                sum_imag = sum_imag + left_real * right_imag + left_imag * right_real
            row_out.append((sum_real, sum_imag))
        result.append(row_out)
    return result


def draw_link_rows(key, part):
    grid_shape = (4, NT, NZ, NY * NX)
    subkeys = jax.random.split(key, 9)
    angle_top = 0.5 * math.pi
    thetas = [jax.random.uniform(subkeys[index], grid_shape, jnp.float32, 0.0, angle_top) for index in range(3)]
    phases = [jax.random.uniform(subkeys[3 + index], grid_shape, jnp.float32, -math.pi, math.pi) for index in range(6)]
    first_rotation = pair_rotation(0, 1, thetas[0], phases[0], phases[1])
    second_rotation = pair_rotation(1, 2, thetas[1], phases[2], phases[3])
    third_rotation = pair_rotation(0, 2, thetas[2], phases[4], phases[5])
    matrix = complex_product(complex_product(first_rotation, second_rotation), third_rotation)
    rows = jnp.stack([jnp.stack([jnp.stack(matrix[row_index][col_index], axis=0) for col_index in range(3)], axis=0) for row_index in range(2)], axis=0)
    return jnp.moveaxis(rows, 3, 0).astype(jnp.float32)


def steps_of(key, dims, cuts, least, top_value):
    level = 1.0
    for dim, shards_of in cuts:
        draws = jax.random.uniform(jax.random.fold_in(jax.random.fold_in(key, 6), dim), (shards_of,), jnp.float32, least / len(cuts), top_value / len(cuts))
        level = level * jnp.repeat(jnp.exp(draws), dims[dim] // shards_of).reshape((-1,) + (1,) * (len(dims) - 1 - dim))
    return level


def bell_draw(key, dims, width, limit, cuts=(), kind=jnp.bfloat16):
    level = steps_of(key, dims, cuts, -0.22, 0.18) if cuts else 1.0
    values = jax.random.normal(key, dims, jnp.float32) * width * level
    return jnp.minimum(jnp.maximum(values, -limit), limit).astype(kind)


def setup_inputs(seed: int = 0) -> dict:
    arg_keys = jax.random.split(jax.random.key(seed), 5)
    source = bell_draw(arg_keys[0], (4, 3, 2, NT, NZ, NYX), 1.0, 6.0, ((3, 12), (4, 16), (5, 4)), jnp.float32)
    link_rows = draw_link_rows(jax.random.fold_in(arg_keys[4], 71), 0)
    clover_diag = jnp.clip(0.6 + 0.79999995 * jax.random.uniform(arg_keys[2], (2, 6, NT, NZ, NYX), jnp.float32) ** steps_of(arg_keys[2], (2, 6, NT, NZ, NYX), ((2, 12), (3, 16), (4, 4)), -0.2, 0.2), 0.6, 1.4)
    clover_off = bell_draw(arg_keys[3], (2, 15, 2, NT, NZ, NYX), 0.12, 0.72, ((3, 12), (4, 16), (5, 4)), jnp.float32)
    return dict(source=source, link_rows=link_rows, clover_diag=clover_diag, clover_off=clover_off)


hop_weight = 0.125
damping = 0.8
UPPER_TABLE = (((1, 0, 1), (0, 0, 1)), ((1, -1, 0), (0, 1, 0)), ((0, 0, 1), (1, 0, -1)), ((0, 1, 0), (1, 1, 0)))
LOWER_TABLE = (((1, 0, -1), (0, 0, -1)), ((1, 1, 0), (0, -1, 0)), ((0, 0, -1), (1, 0, 1)), ((0, 1, 0), (1, 1, 0)))


def spin_mix(half, phase_table):
    rows_out = []
    for source_row, phase_real, phase_imag in phase_table:
        picked = half[source_row]
        real_part = picked[:, 0]
        imag_part = picked[:, 1]
        if phase_imag == 0:
            new_real = phase_real * real_part
            new_imag = phase_real * imag_part
        else:
            new_real = -phase_imag * imag_part
            new_imag = phase_imag * real_part
        rows_out.append(jnp.stack([new_real, new_imag], axis=1))
    return jnp.stack(rows_out, axis=0)


def spin_project(full_spinor, direction, factor):
    upper_half = full_spinor[0:2] + factor * spin_mix(full_spinor[2:4], UPPER_TABLE[direction])
    lower_half = full_spinor[2:4] + factor * spin_mix(full_spinor[0:2], LOWER_TABLE[direction])
    return jnp.concatenate([upper_half, lower_half], axis=0)


def full_link(rows):
    first_row = rows[0]
    second_row = rows[1]
    third = []
    for index in range(3):
        left = (index + 1) % 3
        right = (index + 2) % 3
        real_part = (first_row[left, 0] * second_row[right, 0] - first_row[left, 1] * second_row[right, 1]
                     - first_row[right, 0] * second_row[left, 0] + first_row[right, 1] * second_row[left, 1])
        imag_part = (first_row[left, 0] * second_row[right, 1] + first_row[left, 1] * second_row[right, 0]
                     - first_row[right, 0] * second_row[left, 1] - first_row[right, 1] * second_row[left, 0])
        third.append(jnp.stack([real_part, -imag_part], axis=0))
    return jnp.stack([first_row, second_row, jnp.stack(third, axis=0)], axis=0)


def color_times(link_field, vector, adjoint):
    real_out = 0.0
    imag_out = 0.0
    for column in range(3):
        if adjoint:
            link_real = link_field[column, :, 0]
            link_imag = -link_field[column, :, 1]
        else:
            link_real = link_field[:, column, 0]
            link_imag = link_field[:, column, 1]
        vector_real = vector[:, column, 0][:, None]
        vector_imag = vector[:, column, 1][:, None]
        real_out = real_out + link_real * vector_real - link_imag * vector_imag
        imag_out = imag_out + link_real * vector_imag + link_imag * vector_real
    return jnp.stack([real_out, imag_out], axis=2)


def clover_times(diagonal, offdiag, spinor):
    blocks = spinor.reshape((2, 6) + spinor.shape[2:])
    entries = [blocks[:, index] for index in range(6)]
    result = [diagonal[:, index][:, None] * entries[index] for index in range(6)]
    pair_index = 0
    for row_index in range(6):
        for second in range(row_index + 1, 6):
            real_part = offdiag[:, pair_index, 0]
            imag_part = offdiag[:, pair_index, 1]
            vector = entries[second]
            result[row_index] = result[row_index] + jnp.stack(
                [real_part * vector[:, 0] - imag_part * vector[:, 1], real_part * vector[:, 1] + imag_part * vector[:, 0]], axis=1)
            vector = entries[row_index]
            result[second] = result[second] + jnp.stack(
                [real_part * vector[:, 0] + imag_part * vector[:, 1], real_part * vector[:, 1] - imag_part * vector[:, 0]], axis=1)
            pair_index += 1
    return jnp.stack(result, axis=1).reshape(spinor.shape)


def shifted(field, axis_pos, offset, antiperiodic):
    moved = jnp.roll(field, -offset, axis=axis_pos)
    if antiperiodic:
        count = field.shape[axis_pos]
        edge = count - 1 if offset > 0 else 0
        position = lax.broadcasted_iota(jnp.int32, (count, 1, 1, 1), 0)
        moved = moved * jnp.where(position == edge, -1.0, 1.0)
    return moved


def apply_operator(spinor, rows_view, diagonal, offdiag):
    hopping = jnp.zeros_like(spinor)
    for direction in range(4):
        axis_pos = -1 - direction
        link_field = full_link(rows_view[direction])
        ahead_spinor = shifted(spinor, axis_pos, 1, direction == 3)
        hopping = hopping + spin_project(color_times(link_field, ahead_spinor, False), direction, -1)
        behind = shifted(spinor, axis_pos, -1, direction == 3)
        link_behind = jnp.roll(link_field, 1, axis=axis_pos)
        hopping = hopping + spin_project(color_times(link_behind, behind, True), direction, 1)
    return clover_times(diagonal, offdiag, spinor) - hop_weight * hopping


def reference(source, link_rows, clover_diag, clover_off):
    grid_shape = (NT, NZ, NY, NX)
    spinor_rhs = source.reshape((4, 3, 2) + grid_shape)
    rows_view = link_rows.reshape((4, 2, 3, 2) + grid_shape)
    diagonal = clover_diag.reshape((2, 6) + grid_shape)
    offdiag = clover_off.reshape((2, 15, 2) + grid_shape)
    solution = spinor_rhs
    residual = spinor_rhs
    for sweep_index in range(ITERS):
        residual = spinor_rhs - apply_operator(solution, rows_view, diagonal, offdiag)
        solution = solution + damping * residual
    return solution.reshape(source.shape), residual.reshape(source.shape)
```

```python
import jax
import jax.numpy as jnp
from jax import lax
from jax.experimental import pallas as pl
from jax.experimental.pallas import tpu as pltpu
from jax.sharding import PartitionSpec as P

NX = 32
ITERS = 4
HOP = 0.125
DAMP = 0.8
MESH = pl.DeviceIdType.MESH
AXES = ("ta", "gz", "gy")
F32 = jnp.float32


def lanes():
    return lax.broadcasted_iota(jnp.int32, (8, 128), 1)


def rows():
    return lax.broadcasted_iota(jnp.int32, (8, 128), 0)


def roll_rows(v, by):
    return pltpu.roll(v, by % 8, 0)


def roll_lanes(v, by):
    return pltpu.roll(v, by % 128, 1)


def kernel(
    src_hbm, link_hbm, diag_hbm, off_hbm, sol_ref, res_ref,
    src, link, diag, off, u_re, u_im, c_re, c_im, c_dg, psi,
    t_out, t_in, z_out, z_in, y_out, y_in,
    load_sem, send_sem, recv_sem,
):
    place = [lax.axis_index(a) for a in AXES]
    count = [lax.axis_size(a) for a in AXES]
    ahead = [lax.rem(p + 1, n) for p, n in zip(place, count)]
    back = [lax.rem(p + n - 1, n) for p, n in zip(place, count)]

    barrier = pltpu.get_barrier_semaphore()
    for axis, up, down in zip(AXES, ahead, back):
        for to in (up, down):
            pl.semaphore_signal(barrier, inc=1, device_id={axis: to}, device_id_type=MESH)

    loads = [
        pltpu.make_async_copy(src_hbm, src, load_sem.at[0]),
        pltpu.make_async_copy(link_hbm, link, load_sem.at[1]),
        pltpu.make_async_copy(diag_hbm, diag, load_sem.at[2]),
        pltpu.make_async_copy(off_hbm, off, load_sem.at[3]),
    ]
    for load in loads:
        load.start()

    row, lane = rows(), lanes()
    upper = row < 4
    half = row % 2
    layer = (row // 2) % 2
    sign_j = jnp.where(upper, -1.0, 1.0).astype(F32)

    def times_i(v):
        return roll_rows(v, 4) * sign_j

    def spread(v):
        r = roll_rows(v, 4)
        return jnp.where(upper, v, r), jnp.where(upper, r, v)

    loads[1].wait()
    last = place[0] == count[0] - 1
    t_sign = jnp.where(jnp.logical_and(last, layer == 1), -HOP, HOP).astype(F32)
    conj = jnp.where(upper, 1.0, -1.0).astype(F32)

    def build(mu, weight):
        first = [link[6 * mu + c] for c in range(3)]
        second = [link[6 * mu + 3 + c] for c in range(3)]
        spread_first = [spread(v) for v in first]
        second_i = [times_i(v) for v in second]

        def product(a, b):
            return spread_first[a][0] * second[b] + spread_first[a][1] * second_i[b]

        for c in range(3):
            re, im = spread_first[c]
            u_re[mu, c] = re * weight
            u_im[mu, c] = im * weight
            re, im = spread(second[c])
            u_re[mu, 3 + c] = re * weight
            u_im[mu, 3 + c] = im * weight
            left, right = (c + 1) % 3, (c + 2) % 3
            third = (product(left, right) - product(right, left)) * conj
            re, im = spread(third)
            u_re[mu, 6 + c] = re * weight
            u_im[mu, 6 + c] = im * weight

    for mu in (3, 2, 1, 0):
        build(mu, t_sign if mu == 3 else HOP)

    loads[0].wait()
    for k in range(12):
        psi[k] = src[k]

    loads[2].wait()
    loads[3].wait()
    for k in range(6):
        even, odd = spread(diag[k])
        c_dg[2 * k] = even
        c_dg[2 * k + 1] = odd
    for k in range(30):
        re, im = spread(off[k])
        c_re[k] = re
        c_im[k] = im

    pl.semaphore_wait(barrier, 6)

    def remote(step, kind, way):
        out, into = ((t_out, t_in), (z_out, z_in), (y_out, y_in))[kind]
        to = (back, ahead)[way][kind]
        return pltpu.make_async_remote_copy(
            src_ref=out.at[step, way],
            dst_ref=into.at[step, way],
            send_sem=send_sem.at[step, kind, way],
            recv_sem=recv_sem.at[step, kind, way],
            device_id={AXES[kind]: to},
            device_id_type=MESH,
        )

    def multiply(mu, h, hi):
        out = []
        for spin in range(2):
            for i in range(3):
                total = None
                for j in range(3):
                    term = u_re[mu, 3 * i + j] * h[3 * spin + j] + u_im[mu, 3 * i + j] * hi[3 * spin + j]
                    total = term if total is None else total + term
                out.append(total)
        return out

    def multiply_adjoint(mu, h, hi):
        out = []
        for spin in range(2):
            for i in range(3):
                total = None
                for j in range(3):
                    term = u_re[mu, 3 * j + i] * h[3 * spin + j] - u_im[mu, 3 * j + i] * hi[3 * spin + j]
                    total = term if total is None else total + term
                out.append(total)
        return out

    def project(mu, factor, v, vi):
        def add(a, b, f):
            return a + b if f > 0 else a - b

        h, hi = [], []
        for c in range(3):
            p = [v[3 * s + c] for s in range(4)]
            q = [vi[3 * s + c] for s in range(4)]
            if mu == 0:
                h.append((add(p[0], q[3], factor), add(p[1], q[2], factor)))
                hi.append((add(q[0], p[3], -factor), add(q[1], p[2], -factor)))
            elif mu == 1:
                h.append((add(p[0], p[3], -factor), add(p[1], p[2], factor)))
                hi.append((add(q[0], q[3], -factor), add(q[1], q[2], factor)))
            elif mu == 2:
                h.append((add(p[0], q[2], factor), add(p[1], q[3], -factor)))
                hi.append((add(q[0], p[2], -factor), add(q[1], p[3], factor)))
            else:
                h.append((add(p[0], p[2], factor), add(p[1], p[3], factor)))
                hi.append((add(q[0], q[2], factor), add(q[1], q[3], factor)))
        flat = lambda pairs: [pairs[c][s] for s in range(2) for c in range(3)]
        return flat(h), flat(hi)

    def accumulate(mu, factor, h, acc, acc_i):
        def put(where, at, value, f):
            if where[at] is None:
                where[at] = value if f > 0 else -value
            else:
                where[at] = where[at] + value if f > 0 else where[at] - value

        for c in range(3):
            a, b = h[c], h[3 + c]
            put(acc, c, a, 1)
            put(acc, 3 + c, b, 1)
            if mu == 0:
                put(acc_i, c, b, -factor)
                put(acc_i, 3 + c, a, -factor)
            elif mu == 1:
                put(acc, 6 + c, b, factor)
                put(acc, 9 + c, a, -factor)
            elif mu == 2:
                put(acc_i, c, a, -factor)
                put(acc_i, 3 + c, b, factor)
            else:
                put(acc, 6 + c, a, factor)
                put(acc, 9 + c, b, factor)

    group = lane // 32
    x_place = lane % 32

    def pack_y(h):
        low = jnp.where(
            group < 2,
            jnp.where(group == 0, h[0], roll_lanes(h[1], 32)),
            jnp.where(group == 2, roll_lanes(h[2], 64), roll_lanes(h[3], 96)),
        )
        high = jnp.where(group == 0, h[4], roll_lanes(h[5], 32))
        return low, high

    def step_body(step, carry):
        v = [psi[k] for k in range(12)]
        vi = [times_i(x) for x in v]

        t_fwd, _ = project(3, -1, v, vi)
        for k in range(3):
            t_out[step, 0, k] = jnp.where(layer == 0, t_fwd[k], roll_rows(t_fwd[3 + k], 2))
        remote(step, 0, 0).start()
        h, hi = project(3, 1, v, vi)
        t_bwd = multiply_adjoint(3, h, hi)
        for k in range(3):
            t_out[step, 1, k] = jnp.where(layer == 1, t_bwd[k], roll_rows(t_bwd[3 + k], -2))
        remote(step, 0, 1).start()

        y_fwd, _ = project(1, -1, v, vi)
        low, high = pack_y(y_fwd)
        y_out[step, 0] = jnp.where(half == 0, low, roll_rows(high, 1))
        remote(step, 2, 0).start()
        h, hi = project(1, 1, v, vi)
        y_bwd = multiply_adjoint(1, h, hi)
        y_bwd = [roll_lanes(x, 32) for x in y_bwd]
        low, high = pack_y(y_bwd)
        y_out[step, 1] = jnp.where(half == 1, low, roll_rows(high, -1))
        remote(step, 2, 1).start()

        z_fwd, _ = project(2, -1, v, vi)
        for k in range(6):
            z_out[step, 0, k] = z_fwd[k]
        remote(step, 1, 0).start()
        h, hi = project(2, 1, v, vi)
        z_bwd = multiply_adjoint(2, h, hi)
        for k in range(6):
            z_out[step, 1, k] = z_bwd[k]
        remote(step, 1, 1).start()

        acc = [None] * 12
        acc_i = [None] * 6
        h, _ = project(0, -1, v, vi)
        h = [jnp.where(x_place == 31, roll_lanes(x, 31), roll_lanes(x, -1)) for x in h]
        accumulate(0, -1, multiply(0, h, [times_i(x) for x in h]), acc, acc_i)
        h, hi = project(0, 1, v, vi)
        h = multiply_adjoint(0, h, hi)
        h = [jnp.where(x_place == 0, roll_lanes(x, -31), roll_lanes(x, 1)) for x in h]
        accumulate(0, 1, h, acc, acc_i)

        for b in range(2):
            image = [c_dg[6 * b + i] * v[6 * b + i] for i in range(6)]
            pair = 15 * b
            for i in range(6):
                for j in range(i + 1, 6):
                    re, im = c_re[pair], c_im[pair]
                    image[i] = image[i] + (re * v[6 * b + j] + im * vi[6 * b + j])
                    image[j] = image[j] + (re * v[6 * b + i] - im * vi[6 * b + i])
                    pair += 1
            for i in range(6):
                rest = src[6 * b + i] - image[i]
                k = 6 * b + i
                acc[k] = rest if acc[k] is None else acc[k] + rest

        remote(step, 2, 0).wait_recv()
        got = y_in[step, 0]
        moved = roll_rows(got, 1)
        halo = [
            roll_lanes(moved, 96), roll_lanes(moved, 64), roll_lanes(moved, 32), moved,
            roll_lanes(got, 96), roll_lanes(got, 64),
        ]
        h = []
        for k in range(6):
            r = roll_lanes(y_fwd[k], -32)
            edge = jnp.where(half == 0, roll_rows(r, -1), halo[k])
            h.append(jnp.where(group == 3, edge, r))
        accumulate(1, -1, multiply(1, h, [times_i(x) for x in h]), acc, acc_i)
        remote(step, 2, 1).wait_recv()
        got = y_in[step, 1]
        moved = roll_rows(got, -1)
        halo = [
            moved, roll_lanes(moved, 96), roll_lanes(moved, 64), roll_lanes(moved, 32),
            got, roll_lanes(got, 96),
        ]
        h = []
        for k in range(6):
            r = y_bwd[k]
            edge = jnp.where(half == 1, roll_rows(r, 1), halo[k])
            h.append(jnp.where(group == 0, edge, r))
        accumulate(1, 1, h, acc, acc_i)

        remote(step, 1, 0).wait_recv()
        h = [z_in[step, 0, k] for k in range(6)]
        accumulate(2, -1, multiply(2, h, [times_i(x) for x in h]), acc, acc_i)
        remote(step, 1, 1).wait_recv()
        accumulate(2, 1, [z_in[step, 1, k] for k in range(6)], acc, acc_i)
        for k in range(6):
            acc[6 + k] = acc[6 + k] + times_i(acc_i[k])

        remote(step, 0, 0).wait_recv()
        h = []
        for k in range(6):
            got = t_in[step, 0, k % 3]
            halo = roll_rows(got, 2) if k < 3 else got
            h.append(jnp.where(layer == 0, roll_rows(t_fwd[k], -2), halo))
        accumulate(3, -1, multiply(3, h, [times_i(x) for x in h]), acc, acc_i)
        remote(step, 0, 1).wait_recv()
        h = []
        for k in range(6):
            got = t_in[step, 1, k % 3]
            halo = roll_rows(got, -2) if k < 3 else got
            h.append(jnp.where(layer == 1, roll_rows(t_bwd[k], 2), halo))
        accumulate(3, 1, h, acc, acc_i)

        for k in range(12):
            res_ref[k] = acc[k]
            psi[k] = v[k] + DAMP * acc[k]
        return carry

    lax.fori_loop(0, ITERS, step_body, 0)
    for k in range(12):
        sol_ref[k] = psi[k]

    def drain(step, carry):
        for kind in range(3):
            for way in range(2):
                remote(step, kind, way).wait_send()
        return carry

    lax.fori_loop(0, ITERS, drain, 0)


def body(source, link_rows, clover_diag, clover_off):
    src = source.reshape(12, 8, 128)
    link = link_rows.reshape(24, 8, 128)
    diag = clover_diag.reshape(6, 8, 128)
    off = clover_off.reshape(30, 8, 128)
    field = jax.ShapeDtypeStruct((12, 8, 128), F32)
    vmem = lambda *shape: pltpu.VMEM(shape + (8, 128), F32)
    solution, residual = pl.pallas_call(
        kernel,
        name="clover_steps",
        out_shape=(field, field),
        in_specs=[pl.BlockSpec(memory_space=pl.ANY)] * 4,
        out_specs=[pl.BlockSpec(memory_space=pltpu.VMEM)] * 2,
        scratch_shapes=[
            vmem(12), vmem(24), vmem(6), vmem(30),
            vmem(4, 9), vmem(4, 9), vmem(30), vmem(30), vmem(12), vmem(12),
            vmem(ITERS, 2, 3), vmem(ITERS, 2, 3),
            vmem(ITERS, 2, 6), vmem(ITERS, 2, 6),
            vmem(ITERS, 2), vmem(ITERS, 2),
            pltpu.SemaphoreType.DMA((4,)),
            pltpu.SemaphoreType.DMA((ITERS, 3, 2)),
            pltpu.SemaphoreType.DMA((ITERS, 3, 2)),
        ],
        compiler_params=pltpu.CompilerParams(collective_id=0, has_side_effects=True),
    )(src, link, diag, off)
    return solution.reshape(source.shape), residual.reshape(source.shape)


def solution(mesh):
    in_specs = (
        P(None, None, None, "ta", "gz", "gy"),
        P(None, None, None, None, "ta", "gz", "gy"),
        P(None, None, "ta", "gz", "gy"),
        P(None, None, None, "ta", "gz", "gy"),
    )
    out_specs = (P(None, None, None, "ta", "gz", "gy"), P(None, None, None, "ta", "gz", "gy"))
    return jax.shard_map(body, mesh=mesh, in_specs=in_specs, out_specs=out_specs, check_vma=False)
```

```python
import jax
import jax.numpy as jnp
from jax import lax
from jax.experimental import pallas as pl
from jax.experimental.pallas import tpu as pltpu
from jax.sharding import PartitionSpec as P

NX = 32
ITERS = 4
HOP = 0.125
DAMP = 0.8
MESH = pl.DeviceIdType.MESH
AXES = ("ta", "gz", "gy")
F32 = jnp.float32


def lanes():
    return lax.broadcasted_iota(jnp.int32, (8, 128), 1)


def rows():
    return lax.broadcasted_iota(jnp.int32, (8, 128), 0)


def roll_rows(v, by):
    return pltpu.roll(v, by % 8, 0)


def roll_lanes(v, by):
    return pltpu.roll(v, by % 128, 1)


def kernel(
    src_hbm, link_hbm, diag_hbm, off_hbm, sol_ref, res_ref,
    src, link, diag, off, u_re, u_im, c_re, c_im, c_dg, psi,
    t_out, t_in, z_out, z_in, y_out, y_in,
    load_sem, send_sem, recv_sem,
):
    place = [lax.axis_index(a) for a in AXES]
    count = [lax.axis_size(a) for a in AXES]
    ahead = [lax.rem(p + 1, n) for p, n in zip(place, count)]
    back = [lax.rem(p + n - 1, n) for p, n in zip(place, count)]

    barrier = pltpu.get_barrier_semaphore()
    for axis, up, down in zip(AXES, ahead, back):
        for to in (up, down):
            pl.semaphore_signal(barrier, inc=1, device_id={axis: to}, device_id_type=MESH)

    loads = [
        pltpu.make_async_copy(src_hbm, src, load_sem.at[0]),
        pltpu.make_async_copy(link_hbm, link, load_sem.at[1]),
        pltpu.make_async_copy(diag_hbm, diag, load_sem.at[2]),
        pltpu.make_async_copy(off_hbm, off, load_sem.at[3]),
    ]
    for load in loads:
        load.start()

    row, lane = rows(), lanes()
    upper = row < 4
    half = row % 2
    layer = (row // 2) % 2
    sign_j = jnp.where(upper, -1.0, 1.0).astype(F32)

    def times_i(v):
        return roll_rows(v, 4) * sign_j

    def spread(v):
        r = roll_rows(v, 4)
        return jnp.where(upper, v, r), jnp.where(upper, r, v)

    loads[1].wait()
    last = place[0] == count[0] - 1
    t_sign = jnp.where(jnp.logical_and(last, layer == 1), -HOP, HOP).astype(F32)
    conj = jnp.where(upper, 1.0, -1.0).astype(F32)

    def build(mu, weight):
        first = [link[6 * mu + c] for c in range(3)]
        second = [link[6 * mu + 3 + c] for c in range(3)]
        spread_first = [spread(v) for v in first]
        second_i = [times_i(v) for v in second]

        def product(a, b):
            return spread_first[a][0] * second[b] + spread_first[a][1] * second_i[b]

        for c in range(3):
            re, im = spread_first[c]
            u_re[mu, c] = re * weight
            u_im[mu, c] = im * weight
            re, im = spread(second[c])
            u_re[mu, 3 + c] = re * weight
            u_im[mu, 3 + c] = im * weight
            left, right = (c + 1) % 3, (c + 2) % 3
            third = (product(left, right) - product(right, left)) * conj
            re, im = spread(third)
            u_re[mu, 6 + c] = re * weight
            u_im[mu, 6 + c] = im * weight

    for mu in (3, 2, 1, 0):
        build(mu, t_sign if mu == 3 else HOP)

    loads[0].wait()
    for k in range(12):
        psi[k] = src[k]

    loads[2].wait()
    loads[3].wait()
    for k in range(6):
        even, odd = spread(diag[k])
        c_dg[2 * k] = even
        c_dg[2 * k + 1] = odd
    for k in range(30):
        re, im = spread(off[k])
        c_re[k] = re
        c_im[k] = im

    pl.semaphore_wait(barrier, 6)

    def remote(step, kind, way):
        out, into = ((t_out, t_in), (z_out, z_in), (y_out, y_in))[kind]
        to = (back, ahead)[way][kind]
        return pltpu.make_async_remote_copy(
            src_ref=out.at[step, way],
            dst_ref=into.at[step, way],
            send_sem=send_sem.at[step, kind, way],
            recv_sem=recv_sem.at[step, kind, way],
            device_id={AXES[kind]: to},
            device_id_type=MESH,
        )

    def multiply(mu, h, hi):
        out = []
        for spin in range(2):
            for i in range(3):
                total = None
                for j in range(3):
                    term = u_re[mu, 3 * i + j] * h[3 * spin + j] + u_im[mu, 3 * i + j] * hi[3 * spin + j]
                    total = term if total is None else total + term
                out.append(total)
        return out

    def multiply_adjoint(mu, h, hi):
        out = []
        for spin in range(2):
            for i in range(3):
                total = None
                for j in range(3):
                    term = u_re[mu, 3 * j + i] * h[3 * spin + j] - u_im[mu, 3 * j + i] * hi[3 * spin + j]
                    total = term if total is None else total + term
                out.append(total)
        return out

    def project(mu, factor, v, vi):
        def add(a, b, f):
            return a + b if f > 0 else a - b

        h, hi = [], []
        for c in range(3):
            p = [v[3 * s + c] for s in range(4)]
            q = [vi[3 * s + c] for s in range(4)]
            if mu == 0:
                h.append((add(p[0], q[3], factor), add(p[1], q[2], factor)))
                hi.append((add(q[0], p[3], -factor), add(q[1], p[2], -factor)))
            elif mu == 1:
                h.append((add(p[0], p[3], -factor), add(p[1], p[2], factor)))
                hi.append((add(q[0], q[3], -factor), add(q[1], q[2], factor)))
            elif mu == 2:
                h.append((add(p[0], q[2], factor), add(p[1], q[3], -factor)))
                hi.append((add(q[0], p[2], -factor), add(q[1], p[3], factor)))
            else:
                h.append((add(p[0], p[2], factor), add(p[1], p[3], factor)))
                hi.append((add(q[0], q[2], factor), add(q[1], q[3], factor)))
        flat = lambda pairs: [pairs[c][s] for s in range(2) for c in range(3)]
        return flat(h), flat(hi)

    def accumulate(mu, factor, h, acc, acc_i):
        def put(where, at, value, f):
            if where[at] is None:
                where[at] = value if f > 0 else -value
            else:
                where[at] = where[at] + value if f > 0 else where[at] - value

        for c in range(3):
            a, b = h[c], h[3 + c]
            put(acc, c, a, 1)
            put(acc, 3 + c, b, 1)
            if mu == 0:
                put(acc_i, c, b, -factor)
                put(acc_i, 3 + c, a, -factor)
            elif mu == 1:
                put(acc, 6 + c, b, factor)
                put(acc, 9 + c, a, -factor)
            elif mu == 2:
                put(acc_i, c, a, -factor)
                put(acc_i, 3 + c, b, factor)
            else:
                put(acc, 6 + c, a, factor)
                put(acc, 9 + c, b, factor)

    group = lane // 32
    x_place = lane % 32

    def pack_y(h):
        low = jnp.where(
            group < 2,
            jnp.where(group == 0, h[0], roll_lanes(h[1], 32)),
            jnp.where(group == 2, roll_lanes(h[2], 64), roll_lanes(h[3], 96)),
        )
        high = jnp.where(group == 0, h[4], roll_lanes(h[5], 32))
        return low, high

    def send_t(step, v, vi):
        h, _ = project(3, -1, v, vi)
        for k in range(3):
            t_out[step, 0, k] = jnp.where(layer == 0, h[k], roll_rows(h[3 + k], 2))
        remote(step, 0, 0).start()
        h, hi = project(3, 1, v, vi)
        h = multiply_adjoint(3, h, hi)
        for k in range(3):
            t_out[step, 1, k] = jnp.where(layer == 1, h[k], roll_rows(h[3 + k], -2))
        remote(step, 0, 1).start()

    def step_body(step, final):
        v = [psi[k] for k in range(12)]
        vi = [times_i(x) for x in v]

        y_fwd, _ = project(1, -1, v, vi)
        low, high = pack_y(y_fwd)
        y_out[step, 0] = jnp.where(half == 0, low, roll_rows(high, 1))
        remote(step, 2, 0).start()
        h, hi = project(1, 1, v, vi)
        y_bwd = multiply_adjoint(1, h, hi)
        y_bwd = [roll_lanes(x, 32) for x in y_bwd]
        low, high = pack_y(y_bwd)
        y_out[step, 1] = jnp.where(half == 1, low, roll_rows(high, -1))
        remote(step, 2, 1).start()

        z_fwd, _ = project(2, -1, v, vi)
        for k in range(6):
            z_out[step, 0, k] = z_fwd[k]
        remote(step, 1, 0).start()
        h, hi = project(2, 1, v, vi)
        z_bwd = multiply_adjoint(2, h, hi)
        for k in range(6):
            z_out[step, 1, k] = z_bwd[k]
        remote(step, 1, 1).start()

        acc = [None] * 12
        acc_i = [None] * 6
        h, _ = project(0, -1, v, vi)
        h = [jnp.where(x_place == 31, roll_lanes(x, 31), roll_lanes(x, -1)) for x in h]
        accumulate(0, -1, multiply(0, h, [times_i(x) for x in h]), acc, acc_i)
        h, hi = project(0, 1, v, vi)
        h = multiply_adjoint(0, h, hi)
        h = [jnp.where(x_place == 0, roll_lanes(x, -31), roll_lanes(x, 1)) for x in h]
        accumulate(0, 1, h, acc, acc_i)
        h, _ = project(3, -1, v, vi)
        h = [jnp.where(layer == 0, roll_rows(x, -2), 0.0) for x in h]
        accumulate(3, -1, multiply(3, h, [times_i(x) for x in h]), acc, acc_i)
        h, hi = project(3, 1, v, vi)
        h = multiply_adjoint(3, h, hi)
        h = [jnp.where(layer == 1, roll_rows(x, 2), 0.0) for x in h]
        accumulate(3, 1, h, acc, acc_i)

        for b in range(2):
            image = [c_dg[6 * b + i] * v[6 * b + i] for i in range(6)]
            pair = 15 * b
            for i in range(6):
                for j in range(i + 1, 6):
                    re, im = c_re[pair], c_im[pair]
                    image[i] = image[i] + (re * v[6 * b + j] + im * vi[6 * b + j])
                    image[j] = image[j] + (re * v[6 * b + i] - im * vi[6 * b + i])
                    pair += 1
            for i in range(6):
                k = 6 * b + i
                acc[k] = acc[k] + (src[k] - image[i])

        remote(step, 1, 0).wait_recv()
        h = [z_in[step, 0, k] for k in range(6)]
        accumulate(2, -1, multiply(2, h, [times_i(x) for x in h]), acc, acc_i)
        remote(step, 1, 1).wait_recv()
        accumulate(2, 1, [z_in[step, 1, k] for k in range(6)], acc, acc_i)
        for k in range(6):
            acc[6 + k] = acc[6 + k] + times_i(acc_i[k])

        remote(step, 2, 0).wait_recv()
        got = y_in[step, 0]
        moved = roll_rows(got, 1)
        halo = [
            roll_lanes(moved, 96), roll_lanes(moved, 64), roll_lanes(moved, 32), moved,
            roll_lanes(got, 96), roll_lanes(got, 64),
        ]
        h = []
        for k in range(6):
            r = roll_lanes(y_fwd[k], -32)
            edge = jnp.where(half == 0, roll_rows(r, -1), halo[k])
            h.append(jnp.where(group == 3, edge, r))
        accumulate(1, -1, multiply(1, h, [times_i(x) for x in h]), acc, acc_i)
        remote(step, 2, 1).wait_recv()
        got = y_in[step, 1]
        moved = roll_rows(got, -1)
        halo = [
            moved, roll_lanes(moved, 96), roll_lanes(moved, 64), roll_lanes(moved, 32),
            got, roll_lanes(got, 96),
        ]
        h = []
        for k in range(6):
            r = y_bwd[k]
            edge = jnp.where(half == 1, roll_rows(r, 1), halo[k])
            h.append(jnp.where(group == 0, edge, r))
        accumulate(1, 1, h, acc, acc_i)

        if not final:
            early = [v[k] + DAMP * acc[k] for k in range(12)]
            send_t(step + 1, early, [times_i(x) for x in early])

        remote(step, 0, 0).wait_recv()
        h = []
        for k in range(6):
            got = t_in[step, 0, k % 3]
            halo = roll_rows(got, 2) if k < 3 else got
            h.append(jnp.where(layer == 0, 0.0, halo))
        accumulate(3, -1, multiply(3, h, [times_i(x) for x in h]), acc, acc_i)
        remote(step, 0, 1).wait_recv()
        h = []
        for k in range(6):
            got = t_in[step, 1, k % 3]
            halo = roll_rows(got, -2) if k < 3 else got
            h.append(jnp.where(layer == 1, 0.0, halo))
        accumulate(3, 1, h, acc, acc_i)

        for k in range(12):
            new = v[k] + DAMP * acc[k]
            if final:
                res_ref[k] = acc[k]
                sol_ref[k] = new
            else:
                psi[k] = new

    v = [psi[k] for k in range(12)]
    send_t(0, v, [times_i(x) for x in v])

    def loop_body(step, carry):
        step_body(step, False)
        return carry

    lax.fori_loop(0, ITERS - 1, loop_body, 0)
    step_body(ITERS - 1, True)

    def drain(step, carry):
        for kind in range(3):
            for way in range(2):
                remote(step, kind, way).wait_send()
        return carry

    lax.fori_loop(0, ITERS, drain, 0)


def body(source, link_rows, clover_diag, clover_off):
    src = source.reshape(12, 8, 128)
    link = link_rows.reshape(24, 8, 128)
    diag = clover_diag.reshape(6, 8, 128)
    off = clover_off.reshape(30, 8, 128)
    field = jax.ShapeDtypeStruct((12, 8, 128), F32)
    vmem = lambda *shape: pltpu.VMEM(shape + (8, 128), F32)
    solution, residual = pl.pallas_call(
        kernel,
        name="clover_steps",
        out_shape=(field, field),
        in_specs=[pl.BlockSpec(memory_space=pl.ANY)] * 4,
        out_specs=[pl.BlockSpec(memory_space=pltpu.VMEM)] * 2,
        scratch_shapes=[
            vmem(12), vmem(24), vmem(6), vmem(30),
            vmem(4, 9), vmem(4, 9), vmem(30), vmem(30), vmem(12), vmem(12),
            vmem(ITERS, 2, 3), vmem(ITERS, 2, 3),
            vmem(ITERS, 2, 6), vmem(ITERS, 2, 6),
            vmem(ITERS, 2), vmem(ITERS, 2),
            pltpu.SemaphoreType.DMA((4,)),
            pltpu.SemaphoreType.DMA((ITERS, 3, 2)),
            pltpu.SemaphoreType.DMA((ITERS, 3, 2)),
        ],
        compiler_params=pltpu.CompilerParams(collective_id=0, has_side_effects=True),
    )(src, link, diag, off)
    return solution.reshape(source.shape), residual.reshape(source.shape)


def solution(mesh):
    in_specs = (
        P(None, None, None, "ta", "gz", "gy"),
        P(None, None, None, None, "ta", "gz", "gy"),
        P(None, None, "ta", "gz", "gy"),
        P(None, None, None, "ta", "gz", "gy"),
    )
    out_specs = (P(None, None, None, "ta", "gz", "gy"), P(None, None, None, "ta", "gz", "gy"))
    return jax.shard_map(body, mesh=mesh, in_specs=in_specs, out_specs=out_specs, check_vma=False)
```

```python
import jax
import jax.numpy as jnp
from jax import lax
from jax.experimental import pallas as pl
from jax.experimental.pallas import tpu as pltpu
from jax.sharding import PartitionSpec as P

NX = 32
ITERS = 4
HOP = 0.125
DAMP = 0.8
MESH = pl.DeviceIdType.MESH
AXES = ("ta", "gz", "gy")
F32 = jnp.float32


def lanes():
    return lax.broadcasted_iota(jnp.int32, (8, 128), 1)


def rows():
    return lax.broadcasted_iota(jnp.int32, (8, 128), 0)


def roll_rows(v, by):
    return pltpu.roll(v, by % 8, 0)


def roll_lanes(v, by):
    return pltpu.roll(v, by % 128, 1)


def kernel(
    src_hbm, link_hbm, diag_hbm, off_hbm, sol_ref, res_ref,
    src, link, diag, off, u_re, u_im, c_re, c_im, c_dg, psi,
    out, into, load_sem, send_sem, t_sem, z_sem, y_sem,
):
    loads = [
        pltpu.make_async_copy(src_hbm, src, load_sem.at[0]),
        pltpu.make_async_copy(link_hbm, link, load_sem.at[1]),
        pltpu.make_async_copy(diag_hbm, diag, load_sem.at[2]),
        pltpu.make_async_copy(off_hbm, off, load_sem.at[3]),
    ]
    for load in loads:
        load.start()

    place = [lax.axis_index(a) for a in AXES]
    count = [lax.axis_size(a) for a in AXES]
    ahead = [jnp.where(p == n - 1, 0, p + 1) for p, n in zip(place, count)]
    back = [jnp.where(p == 0, n - 1, p - 1) for p, n in zip(place, count)]

    barrier = pltpu.get_barrier_semaphore()
    for axis, up, down in zip(AXES, ahead, back):
        for to in (up, down):
            pl.semaphore_signal(barrier, inc=1, device_id={axis: to}, device_id_type=MESH)

    row, lane = rows(), lanes()
    upper = row < 4
    half = row % 2
    layer = (row // 2) % 2
    sign_j = jnp.where(upper, -1.0, 1.0).astype(F32)

    def times_i(v):
        return roll_rows(v, 4) * sign_j

    def spread(v):
        r = roll_rows(v, 4)
        return jnp.where(upper, v, r), jnp.where(upper, r, v)

    loads[1].wait()
    last = place[0] == count[0] - 1
    t_sign = jnp.where(jnp.logical_and(last, layer == 1), -HOP, HOP).astype(F32)
    conj = jnp.where(upper, 1.0, -1.0).astype(F32)

    def build(mu, weight):
        first = [link[6 * mu + c] for c in range(3)]
        second = [link[6 * mu + 3 + c] for c in range(3)]
        spread_first = [spread(v) for v in first]
        second_i = [times_i(v) for v in second]

        def product(a, b):
            return spread_first[a][0] * second[b] + spread_first[a][1] * second_i[b]

        for c in range(3):
            re, im = spread_first[c]
            u_re[mu, c] = re * weight
            u_im[mu, c] = im * weight
            re, im = spread(second[c])
            u_re[mu, 3 + c] = re * weight
            u_im[mu, 3 + c] = im * weight
            left, right = (c + 1) % 3, (c + 2) % 3
            third = (product(left, right) - product(right, left)) * conj
            re, im = spread(third)
            u_re[mu, 6 + c] = re * weight
            u_im[mu, 6 + c] = im * weight

    def remote(step, kind, way):
        part = pl.ds((0, 3, 9)[kind], (3, 6, 1)[kind])
        return pltpu.make_async_remote_copy(
            src_ref=out.at[step, way, part],
            dst_ref=into.at[step, way, part],
            send_sem=send_sem,
            recv_sem=(t_sem.at[step, way], z_sem.at[step], y_sem.at[step])[kind],
            device_id={AXES[kind]: (back, ahead)[way][kind]},
            device_id_type=MESH,
        )

    def wait_both(step, kind):
        part = into.at[step, :, pl.ds((0, 3, 9)[kind], (3, 6, 1)[kind])]
        pltpu.make_async_copy(part, part, (None, z_sem.at[step], y_sem.at[step])[kind]).wait()

    def multiply(mu, h, hi):
        out = []
        for spin in range(2):
            for i in range(3):
                total = None
                for j in range(3):
                    term = u_re[mu, 3 * i + j] * h[3 * spin + j] + u_im[mu, 3 * i + j] * hi[3 * spin + j]
                    total = term if total is None else total + term
                out.append(total)
        return out

    def multiply_adjoint(mu, h, hi):
        out = []
        for spin in range(2):
            for i in range(3):
                total = None
                for j in range(3):
                    term = u_re[mu, 3 * j + i] * h[3 * spin + j] - u_im[mu, 3 * j + i] * hi[3 * spin + j]
                    total = term if total is None else total + term
                out.append(total)
        return out

    def project(mu, factor, v, vi):
        def add(a, b, f):
            return a + b if f > 0 else a - b

        h, hi = [], []
        for c in range(3):
            p = [v[3 * s + c] for s in range(4)]
            q = [vi[3 * s + c] for s in range(4)]
            if mu == 0:
                h.append((add(p[0], q[3], factor), add(p[1], q[2], factor)))
                hi.append((add(q[0], p[3], -factor), add(q[1], p[2], -factor)))
            elif mu == 1:
                h.append((add(p[0], p[3], -factor), add(p[1], p[2], factor)))
                hi.append((add(q[0], q[3], -factor), add(q[1], q[2], factor)))
            elif mu == 2:
                h.append((add(p[0], q[2], factor), add(p[1], q[3], -factor)))
                hi.append((add(q[0], p[2], -factor), add(q[1], p[3], factor)))
            else:
                h.append((add(p[0], p[2], factor), add(p[1], p[3], factor)))
                hi.append((add(q[0], q[2], factor), add(q[1], q[3], factor)))
        flat = lambda pairs: [pairs[c][s] for s in range(2) for c in range(3)]
        return flat(h), flat(hi)

    def accumulate(mu, factor, h, acc, acc_i):
        def put(where, at, value, f):
            if where[at] is None:
                where[at] = value if f > 0 else -value
            else:
                where[at] = where[at] + value if f > 0 else where[at] - value

        for c in range(3):
            a, b = h[c], h[3 + c]
            put(acc, c, a, 1)
            put(acc, 3 + c, b, 1)
            if mu == 0:
                put(acc_i, c, b, -factor)
                put(acc_i, 3 + c, a, -factor)
            elif mu == 1:
                put(acc, 6 + c, b, factor)
                put(acc, 9 + c, a, -factor)
            elif mu == 2:
                put(acc_i, c, a, -factor)
                put(acc_i, 3 + c, b, factor)
            else:
                put(acc, 6 + c, a, factor)
                put(acc, 9 + c, b, factor)

    group = lane // 32
    x_place = lane % 32

    def pack_y(h):
        low = jnp.where(
            group < 2,
            jnp.where(group == 0, h[0], roll_lanes(h[1], 32)),
            jnp.where(group == 2, roll_lanes(h[2], 64), roll_lanes(h[3], 96)),
        )
        high = jnp.where(group == 0, h[4], roll_lanes(h[5], 32))
        return low, high

    def send_t(step, v, vi):
        h, _ = project(3, -1, v, vi)
        for k in range(3):
            out[step, 0, k] = jnp.where(layer == 0, h[k], roll_rows(h[3 + k], 2))
        remote(step, 0, 0).start()
        h, hi = project(3, 1, v, vi)
        h = multiply_adjoint(3, h, hi)
        for k in range(3):
            out[step, 1, k] = jnp.where(layer == 1, h[k], roll_rows(h[3 + k], -2))
        remote(step, 0, 1).start()

    def step_body(step, final):
        v = [psi[k] for k in range(12)]
        vi = [times_i(x) for x in v]

        y_fwd, _ = project(1, -1, v, vi)
        low, high = pack_y(y_fwd)
        out[step, 0, 9] = jnp.where(half == 0, low, roll_rows(high, 1))
        remote(step, 2, 0).start()
        h, hi = project(1, 1, v, vi)
        y_bwd = multiply_adjoint(1, h, hi)
        y_bwd = [roll_lanes(x, 32) for x in y_bwd]
        low, high = pack_y(y_bwd)
        out[step, 1, 9] = jnp.where(half == 1, low, roll_rows(high, -1))
        remote(step, 2, 1).start()

        z_fwd, _ = project(2, -1, v, vi)
        for k in range(6):
            out[step, 0, 3 + k] = z_fwd[k]
        remote(step, 1, 0).start()
        h, hi = project(2, 1, v, vi)
        z_bwd = multiply_adjoint(2, h, hi)
        for k in range(6):
            out[step, 1, 3 + k] = z_bwd[k]
        remote(step, 1, 1).start()

        acc = [None] * 12
        acc_i = [None] * 6
        h, _ = project(0, -1, v, vi)
        h = [jnp.where(x_place == 31, roll_lanes(x, 31), roll_lanes(x, -1)) for x in h]
        accumulate(0, -1, multiply(0, h, [times_i(x) for x in h]), acc, acc_i)
        h, hi = project(0, 1, v, vi)
        h = multiply_adjoint(0, h, hi)
        h = [jnp.where(x_place == 0, roll_lanes(x, -31), roll_lanes(x, 1)) for x in h]
        accumulate(0, 1, h, acc, acc_i)
        h, _ = project(3, -1, v, vi)
        h = [jnp.where(layer == 0, roll_rows(x, -2), 0.0) for x in h]
        accumulate(3, -1, multiply(3, h, [times_i(x) for x in h]), acc, acc_i)
        h, hi = project(3, 1, v, vi)
        h = multiply_adjoint(3, h, hi)
        h = [jnp.where(layer == 1, roll_rows(x, 2), 0.0) for x in h]
        accumulate(3, 1, h, acc, acc_i)

        for b in range(2):
            image = [c_dg[6 * b + i] * v[6 * b + i] for i in range(6)]
            pair = 15 * b
            for i in range(6):
                for j in range(i + 1, 6):
                    re, im = c_re[pair], c_im[pair]
                    image[i] = image[i] + (re * v[6 * b + j] + im * vi[6 * b + j])
                    image[j] = image[j] + (re * v[6 * b + i] - im * vi[6 * b + i])
                    pair += 1
            for i in range(6):
                k = 6 * b + i
                acc[k] = acc[k] + (src[k] - image[i])

        wait_both(step, 1)
        h = [into[step, 0, 3 + k] for k in range(6)]
        accumulate(2, -1, multiply(2, h, [times_i(x) for x in h]), acc, acc_i)
        accumulate(2, 1, [into[step, 1, 3 + k] for k in range(6)], acc, acc_i)
        for k in range(6):
            acc[6 + k] = acc[6 + k] + times_i(acc_i[k])

        wait_both(step, 2)
        got = into[step, 0, 9]
        moved = roll_rows(got, 1)
        halo = [
            roll_lanes(moved, 96), roll_lanes(moved, 64), roll_lanes(moved, 32), moved,
            roll_lanes(got, 96), roll_lanes(got, 64),
        ]
        h = []
        for k in range(6):
            r = roll_lanes(y_fwd[k], -32)
            edge = jnp.where(half == 0, roll_rows(r, -1), halo[k])
            h.append(jnp.where(group == 3, edge, r))
        accumulate(1, -1, multiply(1, h, [times_i(x) for x in h]), acc, acc_i)
        got = into[step, 1, 9]
        moved = roll_rows(got, -1)
        halo = [
            moved, roll_lanes(moved, 96), roll_lanes(moved, 64), roll_lanes(moved, 32),
            got, roll_lanes(got, 96),
        ]
        h = []
        for k in range(6):
            r = y_bwd[k]
            edge = jnp.where(half == 1, roll_rows(r, 1), halo[k])
            h.append(jnp.where(group == 0, edge, r))
        accumulate(1, 1, h, acc, acc_i)

        if not final:
            early = [v[k] + DAMP * acc[k] for k in range(12)]
            send_t(step + 1, early, [times_i(x) for x in early])

        remote(step, 0, 0).wait_recv()
        h = []
        for k in range(6):
            got = into[step, 0, k % 3]
            halo = roll_rows(got, 2) if k < 3 else got
            h.append(jnp.where(layer == 0, 0.0, halo))
        accumulate(3, -1, multiply(3, h, [times_i(x) for x in h]), acc, acc_i)
        remote(step, 0, 1).wait_recv()
        h = []
        for k in range(6):
            got = into[step, 1, k % 3]
            halo = roll_rows(got, -2) if k < 3 else got
            h.append(jnp.where(layer == 1, 0.0, halo))
        accumulate(3, 1, h, acc, acc_i)

        for k in range(12):
            new = v[k] + DAMP * acc[k]
            if final:
                res_ref[k] = acc[k]
                sol_ref[k] = new
            else:
                psi[k] = new

    build(3, t_sign)
    loads[0].wait()
    v = [src[k] for k in range(12)]
    for k in range(12):
        psi[k] = v[k]
    pl.semaphore_wait(barrier, 6)
    send_t(0, v, [times_i(x) for x in v])

    for mu in (1, 2, 0):
        build(mu, HOP)
    loads[2].wait()
    loads[3].wait()
    for k in range(6):
        even, odd = spread(diag[k])
        c_dg[2 * k] = even
        c_dg[2 * k + 1] = odd
    for k in range(30):
        re, im = spread(off[k])
        c_re[k] = re
        c_im[k] = im

    def loop_body(step, carry):
        step_body(step, False)
        return carry

    lax.fori_loop(0, ITERS - 1, loop_body, 0)
    step_body(ITERS - 1, True)

    pltpu.make_async_copy(out, out, send_sem).wait()


def body(source, link_rows, clover_diag, clover_off):
    src = source.reshape(12, 8, 128)
    link = link_rows.reshape(24, 8, 128)
    diag = clover_diag.reshape(6, 8, 128)
    off = clover_off.reshape(30, 8, 128)
    field = jax.ShapeDtypeStruct((12, 8, 128), F32)
    vmem = lambda *shape: pltpu.VMEM(shape + (8, 128), F32)
    solution, residual = pl.pallas_call(
        kernel,
        name="clover_steps",
        out_shape=(field, field),
        in_specs=[pl.BlockSpec(memory_space=pl.ANY)] * 4,
        out_specs=[pl.BlockSpec(memory_space=pltpu.VMEM)] * 2,
        scratch_shapes=[
            vmem(12), vmem(24), vmem(6), vmem(30),
            vmem(4, 9), vmem(4, 9), vmem(30), vmem(30), vmem(12), vmem(12),
            vmem(ITERS, 2, 10), vmem(ITERS, 2, 10),
            pltpu.SemaphoreType.DMA((4,)),
            pltpu.SemaphoreType.DMA,
            pltpu.SemaphoreType.DMA((ITERS, 2)),
            pltpu.SemaphoreType.DMA((ITERS,)),
            pltpu.SemaphoreType.DMA((ITERS,)),
        ],
        compiler_params=pltpu.CompilerParams(collective_id=0, has_side_effects=True),
    )(src, link, diag, off)
    return solution.reshape(source.shape), residual.reshape(source.shape)


def solution(mesh):
    in_specs = (
        P(None, None, None, "ta", "gz", "gy"),
        P(None, None, None, None, "ta", "gz", "gy"),
        P(None, None, "ta", "gz", "gy"),
        P(None, None, None, "ta", "gz", "gy"),
    )
    out_specs = (P(None, None, None, "ta", "gz", "gy"), P(None, None, None, "ta", "gz", "gy"))
    return jax.shard_map(body, mesh=mesh, in_specs=in_specs, out_specs=out_specs, check_vma=False)
```

```python
import jax
import jax.numpy as jnp
from jax import lax
from jax.experimental import pallas as pl
from jax.experimental.pallas import tpu as pltpu
from jax.sharding import PartitionSpec as P

NX = 32
ITERS = 4
HOP = 0.125
DAMP = 0.8
MESH = pl.DeviceIdType.MESH
AXES = ("ta", "gz", "gy")
F32 = jnp.float32


def lanes():
    return lax.broadcasted_iota(jnp.int32, (8, 128), 1)


def rows():
    return lax.broadcasted_iota(jnp.int32, (8, 128), 0)


def roll_rows(v, by):
    return pltpu.roll(v, by % 8, 0)


def roll_lanes(v, by):
    return pltpu.roll(v, by % 128, 1)


def kernel(
    src_hbm, link_hbm, diag_hbm, off_hbm, sol_ref, res_ref,
    src, link, diag, off, u_re, u_im, c_re, c_im, c_dg, psi,
    out, into, load_sem, send_sem, t_sem, z_sem, y_sem,
):
    loads = [
        pltpu.make_async_copy(src_hbm, src, load_sem.at[0]),
        pltpu.make_async_copy(link_hbm, link, load_sem.at[1]),
        pltpu.make_async_copy(diag_hbm, diag, load_sem.at[2]),
        pltpu.make_async_copy(off_hbm, off, load_sem.at[3]),
    ]
    for load in loads:
        load.start()

    place = [lax.axis_index(a) for a in AXES]
    count = [lax.axis_size(a) for a in AXES]
    ahead = [jnp.where(p == n - 1, 0, p + 1) for p, n in zip(place, count)]
    back = [jnp.where(p == 0, n - 1, p - 1) for p, n in zip(place, count)]

    barrier = pltpu.get_barrier_semaphore()
    for axis, up, down in zip(AXES, ahead, back):
        for to in (up, down):
            pl.semaphore_signal(barrier, inc=1, device_id={axis: to}, device_id_type=MESH)

    row, lane = rows(), lanes()
    upper = row < 4
    half = row % 2
    layer = (row // 2) % 2
    sign_j = jnp.where(upper, -1.0, 1.0).astype(F32)

    def times_i(v):
        return roll_rows(v, 4) * sign_j

    def spread(v):
        r = roll_rows(v, 4)
        return jnp.where(upper, v, r), jnp.where(upper, r, v)

    loads[1].wait()
    last = place[0] == count[0] - 1
    t_sign = jnp.where(jnp.logical_and(last, layer == 1), -HOP, HOP).astype(F32)
    conj = jnp.where(upper, 1.0, -1.0).astype(F32)

    def build(mu, weight):
        first = [link[6 * mu + c] for c in range(3)]
        second = [link[6 * mu + 3 + c] for c in range(3)]
        spread_first = [spread(v) for v in first]
        second_i = [times_i(v) for v in second]

        def product(a, b):
            return spread_first[a][0] * second[b] + spread_first[a][1] * second_i[b]

        for c in range(3):
            re, im = spread_first[c]
            u_re[mu, c] = re * weight
            u_im[mu, c] = im * weight
            re, im = spread(second[c])
            u_re[mu, 3 + c] = re * weight
            u_im[mu, 3 + c] = im * weight
            left, right = (c + 1) % 3, (c + 2) % 3
            third = (product(left, right) - product(right, left)) * conj
            re, im = spread(third)
            u_re[mu, 6 + c] = re * weight
            u_im[mu, 6 + c] = im * weight

    def remote(step, kind, way):
        part = pl.ds((0, 3, 9)[kind], (3, 6, 1)[kind])
        return pltpu.make_async_remote_copy(
            src_ref=out.at[step, way, part],
            dst_ref=into.at[step, way, part],
            send_sem=send_sem,
            recv_sem=(t_sem.at[step, way], z_sem.at[step], y_sem.at[step])[kind],
            device_id={AXES[kind]: (back, ahead)[way][kind]},
            device_id_type=MESH,
        )

    def wait_both(step, kind):
        part = into.at[step, :, pl.ds((0, 3, 9)[kind], (3, 6, 1)[kind])]
        pltpu.make_async_copy(part, part, (None, z_sem.at[step], y_sem.at[step])[kind]).wait()

    def multiply(mu, h, hi):
        out = []
        for spin in range(2):
            for i in range(3):
                total = None
                for j in range(3):
                    term = u_re[mu, 3 * i + j] * h[3 * spin + j] + u_im[mu, 3 * i + j] * hi[3 * spin + j]
                    total = term if total is None else total + term
                out.append(total)
        return out

    def multiply_adjoint(mu, h, hi):
        out = []
        for spin in range(2):
            for i in range(3):
                total = None
                for j in range(3):
                    term = u_re[mu, 3 * j + i] * h[3 * spin + j] - u_im[mu, 3 * j + i] * hi[3 * spin + j]
                    total = term if total is None else total + term
                out.append(total)
        return out

    def project(mu, factor, v, vi):
        def add(a, b, f):
            return a + b if f > 0 else a - b

        h, hi = [], []
        for c in range(3):
            p = [v[3 * s + c] for s in range(4)]
            q = [vi[3 * s + c] for s in range(4)]
            if mu == 0:
                h.append((add(p[0], q[3], factor), add(p[1], q[2], factor)))
                hi.append((add(q[0], p[3], -factor), add(q[1], p[2], -factor)))
            elif mu == 1:
                h.append((add(p[0], p[3], -factor), add(p[1], p[2], factor)))
                hi.append((add(q[0], q[3], -factor), add(q[1], q[2], factor)))
            elif mu == 2:
                h.append((add(p[0], q[2], factor), add(p[1], q[3], -factor)))
                hi.append((add(q[0], p[2], -factor), add(q[1], p[3], factor)))
            else:
                h.append((add(p[0], p[2], factor), add(p[1], p[3], factor)))
                hi.append((add(q[0], q[2], factor), add(q[1], q[3], factor)))
        flat = lambda pairs: [pairs[c][s] for s in range(2) for c in range(3)]
        return flat(h), flat(hi)

    def accumulate(mu, factor, h, acc, acc_i):
        def put(where, at, value, f):
            if where[at] is None:
                where[at] = value if f > 0 else -value
            else:
                where[at] = where[at] + value if f > 0 else where[at] - value

        for c in range(3):
            a, b = h[c], h[3 + c]
            put(acc, c, a, 1)
            put(acc, 3 + c, b, 1)
            if mu == 0:
                put(acc_i, c, b, -factor)
                put(acc_i, 3 + c, a, -factor)
            elif mu == 1:
                put(acc, 6 + c, b, factor)
                put(acc, 9 + c, a, -factor)
            elif mu == 2:
                put(acc_i, c, a, -factor)
                put(acc_i, 3 + c, b, factor)
            else:
                put(acc, 6 + c, a, factor)
                put(acc, 9 + c, b, factor)

    group = lane // 32
    x_place = lane % 32

    def pack_y(h):
        low = jnp.where(
            group < 2,
            jnp.where(group == 0, h[0], roll_lanes(h[1], 32)),
            jnp.where(group == 2, roll_lanes(h[2], 64), roll_lanes(h[3], 96)),
        )
        high = jnp.where(group == 0, h[4], roll_lanes(h[5], 32))
        return low, high

    def send_t(step, v, vi):
        h, _ = project(3, -1, v, vi)
        for k in range(3):
            out[step, 0, k] = jnp.where(layer == 0, h[k], roll_rows(h[3 + k], 2))
        remote(step, 0, 0).start()
        h, hi = project(3, 1, v, vi)
        h = multiply_adjoint(3, h, hi)
        for k in range(3):
            out[step, 1, k] = jnp.where(layer == 1, h[k], roll_rows(h[3 + k], -2))
        remote(step, 0, 1).start()

    def step_body(step, final):
        v = [psi[k] for k in range(12)]
        vi = [times_i(x) for x in v]

        y_fwd, _ = project(1, -1, v, vi)
        low, high = pack_y(y_fwd)
        out[step, 0, 9] = jnp.where(half == 0, low, roll_rows(high, 1))
        remote(step, 2, 0).start()
        h, hi = project(1, 1, v, vi)
        y_bwd = multiply_adjoint(1, h, hi)
        y_bwd = [roll_lanes(x, 32) for x in y_bwd]
        low, high = pack_y(y_bwd)
        out[step, 1, 9] = jnp.where(half == 1, low, roll_rows(high, -1))
        remote(step, 2, 1).start()

        z_fwd, _ = project(2, -1, v, vi)
        for k in range(6):
            out[step, 0, 3 + k] = z_fwd[k]
        remote(step, 1, 0).start()
        h, hi = project(2, 1, v, vi)
        z_bwd = multiply_adjoint(2, h, hi)
        for k in range(6):
            out[step, 1, 3 + k] = z_bwd[k]
        remote(step, 1, 1).start()

        acc = [None] * 12
        acc_i = [None] * 6
        h, _ = project(0, -1, v, vi)
        h = [jnp.where(x_place == 31, roll_lanes(x, 31), roll_lanes(x, -1)) for x in h]
        accumulate(0, -1, multiply(0, h, [times_i(x) for x in h]), acc, acc_i)
        h, hi = project(0, 1, v, vi)
        h = multiply_adjoint(0, h, hi)
        h = [jnp.where(x_place == 0, roll_lanes(x, -31), roll_lanes(x, 1)) for x in h]
        accumulate(0, 1, h, acc, acc_i)
        h, _ = project(3, -1, v, vi)
        h = [jnp.where(layer == 0, roll_rows(x, -2), 0.0) for x in h]
        accumulate(3, -1, multiply(3, h, [times_i(x) for x in h]), acc, acc_i)
        h, hi = project(3, 1, v, vi)
        h = multiply_adjoint(3, h, hi)
        h = [jnp.where(layer == 1, roll_rows(x, 2), 0.0) for x in h]
        accumulate(3, 1, h, acc, acc_i)

        for b in range(2):
            image = [c_dg[6 * b + i] * v[6 * b + i] for i in range(6)]
            pair = 15 * b
            for i in range(6):
                for j in range(i + 1, 6):
                    re, im = c_re[pair], c_im[pair]
                    image[i] = image[i] + (re * v[6 * b + j] + im * vi[6 * b + j])
                    image[j] = image[j] + (re * v[6 * b + i] - im * vi[6 * b + i])
                    pair += 1
            for i in range(6):
                k = 6 * b + i
                acc[k] = acc[k] + (src[k] - image[i])

        wait_both(step, 1)
        h = [into[step, 0, 3 + k] for k in range(6)]
        accumulate(2, -1, multiply(2, h, [times_i(x) for x in h]), acc, acc_i)
        accumulate(2, 1, [into[step, 1, 3 + k] for k in range(6)], acc, acc_i)
        for k in range(6):
            acc[6 + k] = acc[6 + k] + times_i(acc_i[k])

        wait_both(step, 2)
        got = into[step, 0, 9]
        moved = roll_rows(got, 1)
        halo = [
            roll_lanes(moved, 96), roll_lanes(moved, 64), roll_lanes(moved, 32), moved,
            roll_lanes(got, 96), roll_lanes(got, 64),
        ]
        h = []
        for k in range(6):
            r = roll_lanes(y_fwd[k], -32)
            edge = jnp.where(half == 0, roll_rows(r, -1), halo[k])
            h.append(jnp.where(group == 3, edge, r))
        accumulate(1, -1, multiply(1, h, [times_i(x) for x in h]), acc, acc_i)
        got = into[step, 1, 9]
        moved = roll_rows(got, -1)
        halo = [
            moved, roll_lanes(moved, 96), roll_lanes(moved, 64), roll_lanes(moved, 32),
            got, roll_lanes(got, 96),
        ]
        h = []
        for k in range(6):
            r = y_bwd[k]
            edge = jnp.where(half == 1, roll_rows(r, 1), halo[k])
            h.append(jnp.where(group == 0, edge, r))
        accumulate(1, 1, h, acc, acc_i)

        if not final:
            early = [v[k] + DAMP * acc[k] for k in range(12)]
            send_t(step + 1, early, [times_i(x) for x in early])

        remote(step, 0, 0).wait_recv()
        h = []
        for k in range(6):
            got = into[step, 0, k % 3]
            halo = roll_rows(got, 2) if k < 3 else got
            h.append(jnp.where(layer == 0, 0.0, halo))
        accumulate(3, -1, multiply(3, h, [times_i(x) for x in h]), acc, acc_i)
        remote(step, 0, 1).wait_recv()
        h = []
        for k in range(6):
            got = into[step, 1, k % 3]
            halo = roll_rows(got, -2) if k < 3 else got
            h.append(jnp.where(layer == 1, 0.0, halo))
        accumulate(3, 1, h, acc, acc_i)

        for k in range(12):
            new = v[k] + DAMP * acc[k]
            if final:
                res_ref[k] = acc[k]
                sol_ref[k] = new
            else:
                psi[k] = new

    build(3, t_sign)
    loads[0].wait()
    v = [src[k] for k in range(12)]
    for k in range(12):
        psi[k] = v[k]
    pl.semaphore_wait(barrier, 6)
    send_t(0, v, [times_i(x) for x in v])

    for mu in (1, 2, 0):
        build(mu, HOP)
    loads[2].wait()
    loads[3].wait()
    for k in range(6):
        even, odd = spread(diag[k])
        c_dg[2 * k] = even
        c_dg[2 * k + 1] = odd
    for k in range(30):
        re, im = spread(off[k])
        c_re[k] = re
        c_im[k] = im

    def loop_body(step, carry):
        step_body(step, False)
        return carry

    lax.fori_loop(0, ITERS - 1, loop_body, 0)
    step_body(ITERS - 1, True)

    pltpu.make_async_copy(out, out, send_sem).wait()


def store(sol_ref, res_ref, sol_hbm, res_hbm, sem):
    copies = [
        pltpu.make_async_copy(sol_ref, sol_hbm, sem.at[0]),
        pltpu.make_async_copy(res_ref, res_hbm, sem.at[1]),
    ]
    for copy in copies:
        copy.start()
    for copy in copies:
        copy.wait()


def body(source, link_rows, clover_diag, clover_off):
    src = source.reshape(12, 8, 128)
    link = link_rows.reshape(24, 8, 128)
    diag = clover_diag.reshape(6, 8, 128)
    off = clover_off.reshape(30, 8, 128)
    field = pltpu.VMEM((12, 8, 128), F32)
    vmem = lambda *shape: pltpu.VMEM(shape + (8, 128), F32)
    solution, residual = pl.pallas_call(
        kernel,
        name="clover_steps",
        out_shape=(field, field),
        in_specs=[pl.BlockSpec(memory_space=pl.ANY)] * 4,
        out_specs=[pl.BlockSpec(memory_space=pltpu.VMEM)] * 2,
        scratch_shapes=[
            vmem(12), vmem(24), vmem(6), vmem(30),
            vmem(4, 9), vmem(4, 9), vmem(30), vmem(30), vmem(12), vmem(12),
            vmem(ITERS, 2, 10), vmem(ITERS, 2, 10),
            pltpu.SemaphoreType.DMA((4,)),
            pltpu.SemaphoreType.DMA,
            pltpu.SemaphoreType.DMA((ITERS, 2)),
            pltpu.SemaphoreType.DMA((ITERS,)),
            pltpu.SemaphoreType.DMA((ITERS,)),
        ],
        compiler_params=pltpu.CompilerParams(collective_id=0, has_side_effects=True),
    )(src, link, diag, off)
    field = jax.ShapeDtypeStruct((12, 8, 128), F32)
    solution, residual = pl.pallas_call(
        store,
        name="store",
        out_shape=(field, field),
        in_specs=[pl.BlockSpec(memory_space=pltpu.VMEM)] * 2,
        out_specs=[pl.BlockSpec(memory_space=pl.ANY)] * 2,
        scratch_shapes=[pltpu.SemaphoreType.DMA((2,))],
    )(*(pltpu.with_memory_space_constraint(x, pltpu.VMEM) for x in (solution, residual)))
    return solution.reshape(source.shape), residual.reshape(source.shape)


def solution(mesh):
    in_specs = (
        P(None, None, None, "ta", "gz", "gy"),
        P(None, None, None, None, "ta", "gz", "gy"),
        P(None, None, "ta", "gz", "gy"),
        P(None, None, None, "ta", "gz", "gy"),
    )
    out_specs = (P(None, None, None, "ta", "gz", "gy"), P(None, None, None, "ta", "gz", "gy"))
    return jax.shard_map(body, mesh=mesh, in_specs=in_specs, out_specs=out_specs, check_vma=False)
```

```python
import jax
import jax.numpy as jnp
from jax import lax
from jax.experimental import pallas as pl
from jax.experimental.pallas import tpu as pltpu
from jax.sharding import PartitionSpec as P

NX = 32
ITERS = 4
HOP = 0.125
DAMP = 0.8
MESH = pl.DeviceIdType.MESH
AXES = ("ta", "gz", "gy")
GROUP = 4
F32 = jnp.float32


def lanes():
    return lax.broadcasted_iota(jnp.int32, (8, 128), 1)


def rows():
    return lax.broadcasted_iota(jnp.int32, (8, 128), 0)


def roll_rows(v, by):
    return pltpu.roll(v, by % 8, 0)


def roll_lanes(v, by):
    return pltpu.roll(v, by % 128, 1)


def kernel(
    src_hbm, link_hbm, diag_hbm, off_hbm, sol_ref, res_ref,
    src, link, diag, off, u_re, u_im, c_re, c_im, c_dg, psi, y_fwd, y_bwd,
    out, into, park, load_sem, send_sem, t_sem, z_sem, y_sem,
    ok_sem, park_in, park_ok, park_send,
):
    loads = [
        pltpu.make_async_copy(src_hbm, src, load_sem.at[0]),
        pltpu.make_async_copy(link_hbm, link, load_sem.at[1]),
        pltpu.make_async_copy(diag_hbm, diag, load_sem.at[2]),
        pltpu.make_async_copy(off_hbm, off, load_sem.at[3]),
    ]
    for load in loads:
        load.start()

    place = [lax.axis_index(a) for a in AXES]
    count = [lax.axis_size(a) for a in AXES]
    ahead = [jnp.where(p == n - 1, 0, p + 1) for p, n in zip(place, count)]
    back = [jnp.where(p == 0, n - 1, p - 1) for p, n in zip(place, count)]

    ta, gz, gy = place
    n_ta, n_gz, n_gy = count

    def upward(axis, p):
        return p < (n_ta - 2, n_gz // 2, n_gy - 1)[axis]

    hears = [(upward(a, back[a]), jnp.logical_not(upward(a, place[a]))) for a in range(3)]
    calls = [tuple(jnp.logical_not(h) for h in pair) for pair in hears]
    far = (lax.rem(ta, GROUP) == 0, lax.rem(ta, GROUP) == GROUP - 1)
    first, final_ta = ta == 0, ta == n_ta - 1
    holder = jnp.logical_and(ta == GROUP - 1, gy == 0)

    def beside(axis, way):
        return {AXES[axis]: (back, ahead)[way][axis]}

    barrier = pltpu.get_barrier_semaphore()

    def call(axis, way):
        @pl.when(calls[axis][way])
        def _():
            pl.semaphore_signal(barrier, inc=1, device_id=beside(axis, way), device_id_type=MESH)

    for axis in range(3):
        for way in range(2):
            call(axis, way)

    @pl.when(holder)
    def _():
        for g in range(n_gy):
            for t in (0, n_ta - 1):
                pl.semaphore_signal(barrier, inc=1, device_id={"ta": t, "gy": g}, device_id_type=MESH)

    expected = jnp.logical_or(first, final_ta).astype(jnp.int32)
    for pair in hears:
        for h in pair:
            expected = expected + h.astype(jnp.int32)

    row, lane = rows(), lanes()
    upper = row < 4
    half = row % 2
    layer = (row // 2) % 2
    sign_j = jnp.where(upper, -1.0, 1.0).astype(F32)

    def times_i(v):
        return roll_rows(v, 4) * sign_j

    def spread(v):
        r = roll_rows(v, 4)
        return jnp.where(upper, v, r), jnp.where(upper, r, v)

    loads[1].wait()
    last = place[0] == count[0] - 1
    t_sign = jnp.where(jnp.logical_and(last, layer == 1), -HOP, HOP).astype(F32)
    conj = jnp.where(upper, 1.0, -1.0).astype(F32)

    def build(mu, weight):
        first = [link[6 * mu + c] for c in range(3)]
        second = [link[6 * mu + 3 + c] for c in range(3)]
        spread_first = [spread(v) for v in first]
        second_i = [times_i(v) for v in second]

        def product(a, b):
            return spread_first[a][0] * second[b] + spread_first[a][1] * second_i[b]

        for c in range(3):
            re, im = spread_first[c]
            u_re[mu, c] = re * weight
            u_im[mu, c] = im * weight
            re, im = spread(second[c])
            u_re[mu, 3 + c] = re * weight
            u_im[mu, 3 + c] = im * weight
            left, right = (c + 1) % 3, (c + 2) % 3
            third = (product(left, right) - product(right, left)) * conj
            re, im = spread(third)
            u_re[mu, 6 + c] = re * weight
            u_im[mu, 6 + c] = im * weight

    def remote(step, kind, way):
        part = pl.ds((0, 3, 9)[kind], (3, 6, 1)[kind])
        return pltpu.make_async_remote_copy(
            src_ref=out.at[step, way, part],
            dst_ref=into.at[step, way, part],
            send_sem=send_sem,
            recv_sem=(t_sem.at[step, way], z_sem.at[step % 2], y_sem.at[step % 2])[kind],
            device_id={AXES[kind]: (back, ahead)[way][kind]},
            device_id_type=MESH,
        )

    def wait_both(step, kind):
        part = into.at[step, :, pl.ds((0, 3, 9)[kind], (3, 6, 1)[kind])]
        pltpu.make_async_copy(part, part, (None, z_sem.at[step % 2], y_sem.at[step % 2])[kind]).wait()

    def multiply(mu, h, hi):
        out = []
        for spin in range(2):
            for i in range(3):
                total = None
                for j in range(3):
                    term = u_re[mu, 3 * i + j] * h[3 * spin + j] + u_im[mu, 3 * i + j] * hi[3 * spin + j]
                    total = term if total is None else total + term
                out.append(total)
        return out

    def multiply_adjoint(mu, h, hi):
        out = []
        for spin in range(2):
            for i in range(3):
                total = None
                for j in range(3):
                    term = u_re[mu, 3 * j + i] * h[3 * spin + j] - u_im[mu, 3 * j + i] * hi[3 * spin + j]
                    total = term if total is None else total + term
                out.append(total)
        return out

    def project(mu, factor, v, vi):
        def add(a, b, f):
            return a + b if f > 0 else a - b

        h, hi = [], []
        for c in range(3):
            p = [v[3 * s + c] for s in range(4)]
            q = [vi[3 * s + c] for s in range(4)]
            if mu == 0:
                h.append((add(p[0], q[3], factor), add(p[1], q[2], factor)))
                hi.append((add(q[0], p[3], -factor), add(q[1], p[2], -factor)))
            elif mu == 1:
                h.append((add(p[0], p[3], -factor), add(p[1], p[2], factor)))
                hi.append((add(q[0], q[3], -factor), add(q[1], q[2], factor)))
            elif mu == 2:
                h.append((add(p[0], q[2], factor), add(p[1], q[3], -factor)))
                hi.append((add(q[0], p[2], -factor), add(q[1], p[3], factor)))
            else:
                h.append((add(p[0], p[2], factor), add(p[1], p[3], factor)))
                hi.append((add(q[0], q[2], factor), add(q[1], q[3], factor)))
        flat = lambda pairs: [pairs[c][s] for s in range(2) for c in range(3)]
        return flat(h), flat(hi)

    def accumulate(mu, factor, h, acc, acc_i):
        def put(where, at, value, f):
            if where[at] is None:
                where[at] = value if f > 0 else -value
            else:
                where[at] = where[at] + value if f > 0 else where[at] - value

        for c in range(3):
            a, b = h[c], h[3 + c]
            put(acc, c, a, 1)
            put(acc, 3 + c, b, 1)
            if mu == 0:
                put(acc_i, c, b, -factor)
                put(acc_i, 3 + c, a, -factor)
            elif mu == 1:
                put(acc, 6 + c, b, factor)
                put(acc, 9 + c, a, -factor)
            elif mu == 2:
                put(acc_i, c, a, -factor)
                put(acc_i, 3 + c, b, factor)
            else:
                put(acc, 6 + c, a, factor)
                put(acc, 9 + c, b, factor)

    group = lane // 32
    x_place = lane % 32

    def pack_y(h):
        low = jnp.where(
            group < 2,
            jnp.where(group == 0, h[0], roll_lanes(h[1], 32)),
            jnp.where(group == 2, roll_lanes(h[2], 64), roll_lanes(h[3], 96)),
        )
        high = jnp.where(group == 0, h[4], roll_lanes(h[5], 32))
        return low, high

    def fill_t(step, v, vi, send):
        h, _ = project(3, -1, v, vi)
        for k in range(3):
            out[step, 0, k] = jnp.where(layer == 0, h[k], roll_rows(h[3 + k], 2))
        if send:
            remote(step, 0, 0).start()
        h, hi = project(3, 1, v, vi)
        h = multiply_adjoint(3, h, hi)
        for k in range(3):
            out[step, 1, k] = jnp.where(layer == 1, h[k], roll_rows(h[3 + k], -2))
        if send:
            remote(step, 0, 1).start()

    def fill_yz(step, v, vi, send):
        h, _ = project(1, -1, v, vi)
        low, high = pack_y(h)
        out[step, 0, 9] = jnp.where(half == 0, low, roll_rows(high, 1))
        if send:
            remote(step, 2, 0).start()
        for k in range(6):
            y_fwd[k] = h[k]
        h, hi = project(1, 1, v, vi)
        h = multiply_adjoint(1, h, hi)
        h = [roll_lanes(x, 32) for x in h]
        low, high = pack_y(h)
        out[step, 1, 9] = jnp.where(half == 1, low, roll_rows(high, -1))
        if send:
            remote(step, 2, 1).start()
        for k in range(6):
            y_bwd[k] = h[k]
        h, _ = project(2, -1, v, vi)
        for k in range(6):
            out[step, 0, 3 + k] = h[k]
        if send:
            remote(step, 1, 0).start()
        h, hi = project(2, 1, v, vi)
        h = multiply_adjoint(2, h, hi)
        for k in range(6):
            out[step, 1, 3 + k] = h[k]
        if send:
            remote(step, 1, 1).start()

    def step_body(step, begin, final):
        v = [psi[k] for k in range(12)]
        vi = [times_i(x) for x in v]

        acc = [None] * 12
        acc_i = [None] * 6
        h, _ = project(0, -1, v, vi)
        h = [jnp.where(x_place == 31, roll_lanes(x, 31), roll_lanes(x, -1)) for x in h]
        accumulate(0, -1, multiply(0, h, [times_i(x) for x in h]), acc, acc_i)
        h, hi = project(0, 1, v, vi)
        h = multiply_adjoint(0, h, hi)
        h = [jnp.where(x_place == 0, roll_lanes(x, -31), roll_lanes(x, 1)) for x in h]
        accumulate(0, 1, h, acc, acc_i)
        h, _ = project(3, -1, v, vi)
        h = [jnp.where(layer == 0, roll_rows(x, -2), 0.0) for x in h]
        accumulate(3, -1, multiply(3, h, [times_i(x) for x in h]), acc, acc_i)
        h, hi = project(3, 1, v, vi)
        h = multiply_adjoint(3, h, hi)
        h = [jnp.where(layer == 1, roll_rows(x, 2), 0.0) for x in h]
        accumulate(3, 1, h, acc, acc_i)

        for b in range(2):
            image = [c_dg[6 * b + i] * v[6 * b + i] for i in range(6)]
            pair = 15 * b
            for i in range(6):
                for j in range(i + 1, 6):
                    re, im = c_re[pair], c_im[pair]
                    image[i] = image[i] + (re * v[6 * b + j] + im * vi[6 * b + j])
                    image[j] = image[j] + (re * v[6 * b + i] - im * vi[6 * b + i])
                    pair += 1
            for i in range(6):
                k = 6 * b + i
                acc[k] = acc[k] + (src[k] - image[i])

        wait_both(step, 1)
        h = [into[step, 0, 3 + k] for k in range(6)]
        accumulate(2, -1, multiply(2, h, [times_i(x) for x in h]), acc, acc_i)
        accumulate(2, 1, [into[step, 1, 3 + k] for k in range(6)], acc, acc_i)
        for k in range(6):
            acc[6 + k] = acc[6 + k] + times_i(acc_i[k])

        wait_both(step, 2)
        got = into[step, 0, 9]
        moved = roll_rows(got, 1)
        halo = [
            roll_lanes(moved, 96), roll_lanes(moved, 64), roll_lanes(moved, 32), moved,
            roll_lanes(got, 96), roll_lanes(got, 64),
        ]
        h = []
        for k in range(6):
            r = roll_lanes(y_fwd[k], -32)
            edge = jnp.where(half == 0, roll_rows(r, -1), halo[k])
            h.append(jnp.where(group == 3, edge, r))
        accumulate(1, -1, multiply(1, h, [times_i(x) for x in h]), acc, acc_i)
        got = into[step, 1, 9]
        moved = roll_rows(got, -1)
        halo = [
            moved, roll_lanes(moved, 96), roll_lanes(moved, 64), roll_lanes(moved, 32),
            got, roll_lanes(got, 96),
        ]
        h = []
        for k in range(6):
            r = y_bwd[k]
            edge = jnp.where(half == 1, roll_rows(r, 1), halo[k])
            h.append(jnp.where(group == 0, edge, r))
        accumulate(1, 1, h, acc, acc_i)

        if begin:
            @pl.when(first)
            def _():
                pl.semaphore_wait(ok_sem.at[0, 0], 1)

            @pl.when(jnp.logical_and(far[1], calls[0][1]))
            def _():
                pl.semaphore_wait(ok_sem.at[0, 1], 1)
                remote(0, 0, 1).start()

        if not final:
            early = [v[k] + DAMP * acc[k] for k in range(12)]
            fill_t(step + 1, early, [times_i(x) for x in early], True)

        remote(step, 0, 0).wait_recv()
        h = []
        for k in range(6):
            got = into[step, 0, k % 3]
            halo = roll_rows(got, 2) if k < 3 else got
            h.append(jnp.where(layer == 0, 0.0, halo))
        accumulate(3, -1, multiply(3, h, [times_i(x) for x in h]), acc, acc_i)
        remote(step, 0, 1).wait_recv()
        h = []
        for k in range(6):
            got = into[step, 1, k % 3]
            halo = roll_rows(got, -2) if k < 3 else got
            h.append(jnp.where(layer == 1, 0.0, halo))
        accumulate(3, 1, h, acc, acc_i)

        new = [v[k] + DAMP * acc[k] for k in range(12)]
        if final:
            for k in range(12):
                res_ref[k] = acc[k]
                sol_ref[k] = new[k]
        else:
            for k in range(12):
                psi[k] = new[k]
            fill_yz(step + 1, new, [times_i(x) for x in new], True)

    build(3, t_sign)
    loads[0].wait()
    v = [src[k] for k in range(12)]
    vi = [times_i(x) for x in v]
    for k in range(12):
        psi[k] = v[k]
    fill_t(0, v, vi, False)
    for mu in (1, 2, 0):
        build(mu, HOP)
    fill_yz(0, v, vi, False)
    pl.semaphore_wait(barrier, expected)

    def answer(axis, way):
        @pl.when(hears[axis][way])
        def _():
            pl.semaphore_signal(
                ok_sem.at[axis, 1 - way], inc=1, device_id=beside(axis, way), device_id_type=MESH
            )

    for axis in range(3):
        for way in range(2):
            answer(axis, way)

    @pl.when(final_ta)
    def _():
        pl.semaphore_signal(
            park_ok.at[gy], inc=1, device_id={"ta": GROUP - 1, "gy": 0}, device_id_type=MESH
        )

    def open_to(kind, way):
        @pl.when(calls[kind][way])
        def _():
            pl.semaphore_wait(ok_sem.at[kind, way], 1)

        remote(0, kind, way).start()

    for way in range(2):
        @pl.when(jnp.logical_and(far[way], hears[0][way]))
        def _(way=way):
            remote(0, 0, way).start()

    @pl.when(first)
    def _():
        pltpu.make_async_remote_copy(
            src_ref=out.at[0, 0, pl.ds(0, 3)],
            dst_ref=park.at[gy],
            send_sem=send_sem,
            recv_sem=park_in.at[gy],
            device_id={"ta": GROUP - 1, "gy": 0},
            device_id_type=MESH,
        ).start()

    for kind in (2, 1):
        for way in range(2):
            open_to(kind, way)
    for way in range(2):
        @pl.when(jnp.logical_not(far[way]))
        def _(way=way):
            open_to(0, way)

    def hand_on(g):
        return pltpu.make_async_remote_copy(
            src_ref=park.at[g],
            dst_ref=into.at[0, 0, pl.ds(0, 3)],
            send_sem=park_send,
            recv_sem=t_sem.at[0, 0],
            device_id={"ta": n_ta - 1, "gy": g},
            device_id_type=MESH,
        )

    loads[2].wait()
    loads[3].wait()
    for k in range(6):
        even, odd = spread(diag[k])
        c_dg[2 * k] = even
        c_dg[2 * k + 1] = odd
    for k in range(30):
        re, im = spread(off[k])
        c_re[k] = re
        c_im[k] = im

    step_body(0, True, False)

    @pl.when(holder)
    def _():
        for g in range(n_gy):
            pltpu.make_async_copy(park.at[g], park.at[g], park_in.at[g]).wait()
            pl.semaphore_wait(park_ok.at[g], 1)
            hand_on(g).start()

    def loop_body(step, carry):
        step_body(step, False, False)
        return carry

    lax.fori_loop(1, ITERS - 1, loop_body, 0)
    step_body(ITERS - 1, False, True)

    @pl.when(holder)
    def _():
        pltpu.make_async_copy(park, park, park_send).wait()

    pltpu.make_async_copy(out, out, send_sem).wait()


def store(sol_ref, res_ref, sol_hbm, res_hbm, sem):
    copies = [
        pltpu.make_async_copy(sol_ref, sol_hbm, sem.at[0]),
        pltpu.make_async_copy(res_ref, res_hbm, sem.at[1]),
    ]
    for copy in copies:
        copy.start()
    for copy in copies:
        copy.wait()


def body(source, link_rows, clover_diag, clover_off):
    src = source.reshape(12, 8, 128)
    link = link_rows.reshape(24, 8, 128)
    diag = clover_diag.reshape(6, 8, 128)
    off = clover_off.reshape(30, 8, 128)
    field = pltpu.VMEM((12, 8, 128), F32)
    n_gy = lax.axis_size("gy")
    vmem = lambda *shape: pltpu.VMEM(shape + (8, 128), F32)
    solution, residual = pl.pallas_call(
        kernel,
        name="clover_steps",
        out_shape=(field, field),
        in_specs=[pl.BlockSpec(memory_space=pl.ANY)] * 4,
        out_specs=[pl.BlockSpec(memory_space=pltpu.VMEM)] * 2,
        scratch_shapes=[
            vmem(12), vmem(24), vmem(6), vmem(30),
            vmem(4, 9), vmem(4, 9), vmem(30), vmem(30), vmem(12), vmem(12), vmem(6), vmem(6),
            vmem(ITERS, 2, 10), vmem(ITERS, 2, 10), vmem(n_gy, 3),
            pltpu.SemaphoreType.DMA((4,)),
            pltpu.SemaphoreType.DMA,
            pltpu.SemaphoreType.DMA((ITERS, 2)),
            pltpu.SemaphoreType.DMA((2,)),
            pltpu.SemaphoreType.DMA((2,)),
            pltpu.SemaphoreType.REGULAR((3, 2)),
            pltpu.SemaphoreType.DMA((n_gy,)),
            pltpu.SemaphoreType.REGULAR((n_gy,)),
            pltpu.SemaphoreType.DMA,
        ],
        compiler_params=pltpu.CompilerParams(collective_id=0, has_side_effects=True),
    )(src, link, diag, off)
    field = jax.ShapeDtypeStruct((12, 8, 128), F32)
    solution, residual = pl.pallas_call(
        store,
        name="store",
        out_shape=(field, field),
        in_specs=[pl.BlockSpec(memory_space=pltpu.VMEM)] * 2,
        out_specs=[pl.BlockSpec(memory_space=pl.ANY)] * 2,
        scratch_shapes=[pltpu.SemaphoreType.DMA((2,))],
    )(*(pltpu.with_memory_space_constraint(x, pltpu.VMEM) for x in (solution, residual)))
    return solution.reshape(source.shape), residual.reshape(source.shape)


def solution(mesh):
    in_specs = (
        P(None, None, None, "ta", "gz", "gy"),
        P(None, None, None, None, "ta", "gz", "gy"),
        P(None, None, "ta", "gz", "gy"),
        P(None, None, None, "ta", "gz", "gy"),
    )
    out_specs = (P(None, None, None, "ta", "gz", "gy"), P(None, None, None, "ta", "gz", "gy"))
    return jax.shard_map(body, mesh=mesh, in_specs=in_specs, out_specs=out_specs, check_vma=False)
```

```python
import jax
import jax.numpy as jnp
from jax import lax
from jax.experimental import pallas as pl
from jax.experimental.pallas import tpu as pltpu
from jax.sharding import PartitionSpec as P

NX = 32
ITERS = 4
HOP = 0.125
DAMP = 0.8
MESH = pl.DeviceIdType.MESH
AXES = ("ta", "gz", "gy")
GROUP = 4
F32 = jnp.float32


def lanes():
    return lax.broadcasted_iota(jnp.int32, (8, 128), 1)


def rows():
    return lax.broadcasted_iota(jnp.int32, (8, 128), 0)


def roll_rows(v, by):
    return pltpu.roll(v, by % 8, 0)


def roll_lanes(v, by):
    return pltpu.roll(v, by % 128, 1)


def kernel(
    src_hbm, link_hbm, diag_hbm, off_hbm, sol_ref, res_ref,
    src, link, diag, off, u_re, u_im, c_re, c_im, c_dg, psi, y_fwd, y_bwd,
    out, into, park, load_sem, send_sem, t_sem, z_sem, y_sem,
    ok_sem, park_in, park_ok, park_send,
):
    loads = [
        pltpu.make_async_copy(src_hbm, src, load_sem.at[0]),
        pltpu.make_async_copy(link_hbm, link, load_sem.at[1]),
        pltpu.make_async_copy(diag_hbm, diag, load_sem.at[2]),
        pltpu.make_async_copy(off_hbm, off, load_sem.at[3]),
    ]
    for load in loads:
        load.start()

    place = [lax.axis_index(a) for a in AXES]
    count = [lax.axis_size(a) for a in AXES]
    ahead = [jnp.where(p == n - 1, 0, p + 1) for p, n in zip(place, count)]
    back = [jnp.where(p == 0, n - 1, p - 1) for p, n in zip(place, count)]

    ta, gz, gy = place
    n_ta, n_gz, n_gy = count

    def upward(axis, p):
        if axis == 1:
            return jnp.logical_and(p % 2 == 1, p < n_gz - 1)
        return p < (n_ta - 2, None, n_gy - 1)[axis]

    hears = [(upward(a, back[a]), jnp.logical_not(upward(a, place[a]))) for a in range(3)]
    calls = [tuple(jnp.logical_not(h) for h in pair) for pair in hears]
    far = (lax.rem(ta, GROUP) == 0, lax.rem(ta, GROUP) == GROUP - 1)
    early = jnp.logical_or(ta == 0, ta == GROUP - 1)
    late = jnp.logical_or(ta == n_ta - 1, ta == GROUP)
    onward = jnp.logical_or(ta == GROUP - 1, ta == GROUP).astype(jnp.int32)
    holds = (jnp.logical_and(ta == GROUP - 1, gy == 0), jnp.logical_and(ta == 0, gy == n_gy - 1))
    holder_of = {
        "ta": jnp.where(onward == 1, 0, GROUP - 1), "gy": jnp.where(onward == 1, n_gy - 1, 0)
    }
    ends = ((0, n_ta - 1), (GROUP - 1, GROUP))

    def beside(axis, way):
        return {AXES[axis]: (back, ahead)[way][axis]}

    barrier = pltpu.get_barrier_semaphore()

    def call(axis, way):
        @pl.when(calls[axis][way])
        def _():
            pl.semaphore_signal(barrier, inc=1, device_id=beside(axis, way), device_id_type=MESH)

    for axis in range(3):
        for way in range(2):
            call(axis, way)

    for way in range(2):
        @pl.when(holds[way])
        def _(way=way):
            for g in range(n_gy):
                for t in ends[way]:
                    pl.semaphore_signal(barrier, inc=1, device_id={"ta": t, "gy": g}, device_id_type=MESH)

    expected = jnp.logical_or(early, late).astype(jnp.int32)
    for pair in hears:
        for h in pair:
            expected = expected + h.astype(jnp.int32)
    pl.semaphore_wait(barrier, expected)

    def answer(axis, way):
        @pl.when(hears[axis][way])
        def _():
            pl.semaphore_signal(
                ok_sem.at[axis, 1 - way], inc=1, device_id=beside(axis, way), device_id_type=MESH
            )

    for axis in range(3):
        for way in range(2):
            answer(axis, way)

    @pl.when(late)
    def _():
        pl.semaphore_signal(park_ok.at[gy], inc=1, device_id=holder_of, device_id_type=MESH)

    row, lane = rows(), lanes()
    upper = row < 4
    half = row % 2
    layer = (row // 2) % 2
    sign_j = jnp.where(upper, -1.0, 1.0).astype(F32)

    def times_i(v):
        return roll_rows(v, 4) * sign_j

    def spread(v):
        r = roll_rows(v, 4)
        return jnp.where(upper, v, r), jnp.where(upper, r, v)

    loads[1].wait()
    last = place[0] == count[0] - 1
    t_sign = jnp.where(jnp.logical_and(last, layer == 1), -HOP, HOP).astype(F32)
    conj = jnp.where(upper, 1.0, -1.0).astype(F32)

    def build(mu, weight):
        first = [link[6 * mu + c] for c in range(3)]
        second = [link[6 * mu + 3 + c] for c in range(3)]
        spread_first = [spread(v) for v in first]
        second_i = [times_i(v) for v in second]

        def product(a, b):
            return spread_first[a][0] * second[b] + spread_first[a][1] * second_i[b]

        for c in range(3):
            re, im = spread_first[c]
            u_re[mu, c] = re * weight
            u_im[mu, c] = im * weight
            re, im = spread(second[c])
            u_re[mu, 3 + c] = re * weight
            u_im[mu, 3 + c] = im * weight
            left, right = (c + 1) % 3, (c + 2) % 3
            third = (product(left, right) - product(right, left)) * conj
            re, im = spread(third)
            u_re[mu, 6 + c] = re * weight
            u_im[mu, 6 + c] = im * weight

    def remote(step, kind, way):
        part = pl.ds((0, 3, 9)[kind], (3, 6, 1)[kind])
        return pltpu.make_async_remote_copy(
            src_ref=out.at[step, way, part],
            dst_ref=into.at[step, way, part],
            send_sem=send_sem,
            recv_sem=(t_sem.at[step, way], z_sem.at[step % 2], y_sem.at[step % 2])[kind],
            device_id={AXES[kind]: (back, ahead)[way][kind]},
            device_id_type=MESH,
        )

    def wait_both(step, kind):
        part = into.at[step, :, pl.ds((0, 3, 9)[kind], (3, 6, 1)[kind])]
        pltpu.make_async_copy(part, part, (None, z_sem.at[step % 2], y_sem.at[step % 2])[kind]).wait()

    def multiply(mu, h, hi):
        out = []
        for spin in range(2):
            for i in range(3):
                total = None
                for j in range(3):
                    term = u_re[mu, 3 * i + j] * h[3 * spin + j] + u_im[mu, 3 * i + j] * hi[3 * spin + j]
                    total = term if total is None else total + term
                out.append(total)
        return out

    def multiply_adjoint(mu, h, hi):
        out = []
        for spin in range(2):
            for i in range(3):
                total = None
                for j in range(3):
                    term = u_re[mu, 3 * j + i] * h[3 * spin + j] - u_im[mu, 3 * j + i] * hi[3 * spin + j]
                    total = term if total is None else total + term
                out.append(total)
        return out

    def project(mu, factor, v, vi):
        def add(a, b, f):
            return a + b if f > 0 else a - b

        h, hi = [], []
        for c in range(3):
            p = [v[3 * s + c] for s in range(4)]
            q = [vi[3 * s + c] for s in range(4)]
            if mu == 0:
                h.append((add(p[0], q[3], factor), add(p[1], q[2], factor)))
                hi.append((add(q[0], p[3], -factor), add(q[1], p[2], -factor)))
            elif mu == 1:
                h.append((add(p[0], p[3], -factor), add(p[1], p[2], factor)))
                hi.append((add(q[0], q[3], -factor), add(q[1], q[2], factor)))
            elif mu == 2:
                h.append((add(p[0], q[2], factor), add(p[1], q[3], -factor)))
                hi.append((add(q[0], p[2], -factor), add(q[1], p[3], factor)))
            else:
                h.append((add(p[0], p[2], factor), add(p[1], p[3], factor)))
                hi.append((add(q[0], q[2], factor), add(q[1], q[3], factor)))
        flat = lambda pairs: [pairs[c][s] for s in range(2) for c in range(3)]
        return flat(h), flat(hi)

    def accumulate(mu, factor, h, acc, acc_i):
        def put(where, at, value, f):
            if where[at] is None:
                where[at] = value if f > 0 else -value
            else:
                where[at] = where[at] + value if f > 0 else where[at] - value

        for c in range(3):
            a, b = h[c], h[3 + c]
            put(acc, c, a, 1)
            put(acc, 3 + c, b, 1)
            if mu == 0:
                put(acc_i, c, b, -factor)
                put(acc_i, 3 + c, a, -factor)
            elif mu == 1:
                put(acc, 6 + c, b, factor)
                put(acc, 9 + c, a, -factor)
            elif mu == 2:
                put(acc_i, c, a, -factor)
                put(acc_i, 3 + c, b, factor)
            else:
                put(acc, 6 + c, a, factor)
                put(acc, 9 + c, b, factor)

    group = lane // 32
    x_place = lane % 32

    def pack_y(h):
        low = jnp.where(
            group < 2,
            jnp.where(group == 0, h[0], roll_lanes(h[1], 32)),
            jnp.where(group == 2, roll_lanes(h[2], 64), roll_lanes(h[3], 96)),
        )
        high = jnp.where(group == 0, h[4], roll_lanes(h[5], 32))
        return low, high

    def leave(step, way):
        return pltpu.make_async_remote_copy(
            src_ref=out.at[step, way, pl.ds(0, 3)],
            dst_ref=park.at[step, gy],
            send_sem=send_sem,
            recv_sem=park_in.at[step, gy],
            device_id=holder_of,
            device_id_type=MESH,
        )

    def hand_on(way):
        @pl.when(holds[way])
        def _():
            for step in range(2):
                for g in range(n_gy):
                    got = park.at[step, g]
                    pltpu.make_async_copy(got, got, park_in.at[step, g]).wait()
                    if step == 0:
                        pl.semaphore_wait(park_ok.at[g], 1)
                    pltpu.make_async_remote_copy(
                        src_ref=got,
                        dst_ref=into.at[step, way, pl.ds(0, 3)],
                        send_sem=park_send,
                        recv_sem=t_sem.at[step, way],
                        device_id={"ta": ends[way][1], "gy": g},
                        device_id_type=MESH,
                    ).start()

    def fill_t(step, v, vi, send):
        h, _ = project(3, -1, v, vi)
        for k in range(3):
            out[step, 0, k] = jnp.where(layer == 0, h[k], roll_rows(h[3 + k], 2))
        if send:
            send(step, 0)
        h, hi = project(3, 1, v, vi)
        h = multiply_adjoint(3, h, hi)
        for k in range(3):
            out[step, 1, k] = jnp.where(layer == 1, h[k], roll_rows(h[3 + k], -2))
        if send:
            send(step, 1)

    def send_t(step, way):
        remote(step, 0, way).start()

    def send_or_leave(step, way):
        mine = jnp.logical_and(early, onward == way)

        @pl.when(jnp.logical_not(mine))
        def _():
            remote(step, 0, way).start()

        @pl.when(mine)
        def _():
            leave(step, way).start()

    def fill_yz(step, v, vi, send):
        h, _ = project(1, -1, v, vi)
        low, high = pack_y(h)
        out[step, 0, 9] = jnp.where(half == 0, low, roll_rows(high, 1))
        if send:
            remote(step, 2, 0).start()
        for k in range(6):
            y_fwd[k] = h[k]
        h, hi = project(1, 1, v, vi)
        h = multiply_adjoint(1, h, hi)
        h = [roll_lanes(x, 32) for x in h]
        low, high = pack_y(h)
        out[step, 1, 9] = jnp.where(half == 1, low, roll_rows(high, -1))
        if send:
            remote(step, 2, 1).start()
        for k in range(6):
            y_bwd[k] = h[k]
        h, _ = project(2, -1, v, vi)
        for k in range(6):
            out[step, 0, 3 + k] = h[k]
        if send:
            remote(step, 1, 0).start()
        h, hi = project(2, 1, v, vi)
        h = multiply_adjoint(2, h, hi)
        for k in range(6):
            out[step, 1, 3 + k] = h[k]
        if send:
            remote(step, 1, 1).start()

    def step_body(step, begin, final):
        v = [psi[k] for k in range(12)]
        vi = [times_i(x) for x in v]

        acc = [None] * 12
        acc_i = [None] * 6
        h, _ = project(0, -1, v, vi)
        h = [jnp.where(x_place == 31, roll_lanes(x, 31), roll_lanes(x, -1)) for x in h]
        accumulate(0, -1, multiply(0, h, [times_i(x) for x in h]), acc, acc_i)
        h, hi = project(0, 1, v, vi)
        h = multiply_adjoint(0, h, hi)
        h = [jnp.where(x_place == 0, roll_lanes(x, -31), roll_lanes(x, 1)) for x in h]
        accumulate(0, 1, h, acc, acc_i)
        h, _ = project(3, -1, v, vi)
        h = [jnp.where(layer == 0, roll_rows(x, -2), 0.0) for x in h]
        accumulate(3, -1, multiply(3, h, [times_i(x) for x in h]), acc, acc_i)
        h, hi = project(3, 1, v, vi)
        h = multiply_adjoint(3, h, hi)
        h = [jnp.where(layer == 1, roll_rows(x, 2), 0.0) for x in h]
        accumulate(3, 1, h, acc, acc_i)

        for b in range(2):
            image = [c_dg[6 * b + i] * v[6 * b + i] for i in range(6)]
            pair = 15 * b
            for i in range(6):
                for j in range(i + 1, 6):
                    re, im = c_re[pair], c_im[pair]
                    image[i] = image[i] + (re * v[6 * b + j] + im * vi[6 * b + j])
                    image[j] = image[j] + (re * v[6 * b + i] - im * vi[6 * b + i])
                    pair += 1
            for i in range(6):
                k = 6 * b + i
                acc[k] = acc[k] + (src[k] - image[i])

        wait_both(step, 1)
        h = [into[step, 0, 3 + k] for k in range(6)]
        accumulate(2, -1, multiply(2, h, [times_i(x) for x in h]), acc, acc_i)
        accumulate(2, 1, [into[step, 1, 3 + k] for k in range(6)], acc, acc_i)
        for k in range(6):
            acc[6 + k] = acc[6 + k] + times_i(acc_i[k])

        wait_both(step, 2)
        got = into[step, 0, 9]
        moved = roll_rows(got, 1)
        halo = [
            roll_lanes(moved, 96), roll_lanes(moved, 64), roll_lanes(moved, 32), moved,
            roll_lanes(got, 96), roll_lanes(got, 64),
        ]
        h = []
        for k in range(6):
            r = roll_lanes(y_fwd[k], -32)
            edge = jnp.where(half == 0, roll_rows(r, -1), halo[k])
            h.append(jnp.where(group == 3, edge, r))
        accumulate(1, -1, multiply(1, h, [times_i(x) for x in h]), acc, acc_i)
        got = into[step, 1, 9]
        moved = roll_rows(got, -1)
        halo = [
            moved, roll_lanes(moved, 96), roll_lanes(moved, 64), roll_lanes(moved, 32),
            got, roll_lanes(got, 96),
        ]
        h = []
        for k in range(6):
            r = y_bwd[k]
            edge = jnp.where(half == 1, roll_rows(r, 1), halo[k])
            h.append(jnp.where(group == 0, edge, r))
        accumulate(1, 1, h, acc, acc_i)

        if begin:
            @pl.when(jnp.logical_and(jnp.logical_and(far[1], calls[0][1]), jnp.logical_not(early)))
            def _():
                pl.semaphore_wait(ok_sem.at[0, 1], 1)
                remote(0, 0, 1).start()

        if not final:
            part = [v[k] + DAMP * acc[k] for k in range(12)]
            fill_t(step + 1, part, [times_i(x) for x in part], send_or_leave if begin else send_t)
        if begin:
            hand_on(1)

        remote(step, 0, 0).wait_recv()
        h = []
        for k in range(6):
            got = into[step, 0, k % 3]
            halo = roll_rows(got, 2) if k < 3 else got
            h.append(jnp.where(layer == 0, 0.0, halo))
        accumulate(3, -1, multiply(3, h, [times_i(x) for x in h]), acc, acc_i)
        remote(step, 0, 1).wait_recv()
        h = []
        for k in range(6):
            got = into[step, 1, k % 3]
            halo = roll_rows(got, -2) if k < 3 else got
            h.append(jnp.where(layer == 1, 0.0, halo))
        accumulate(3, 1, h, acc, acc_i)

        new = [v[k] + DAMP * acc[k] for k in range(12)]
        if final:
            for k in range(12):
                res_ref[k] = acc[k]
                sol_ref[k] = new[k]
        else:
            for k in range(12):
                psi[k] = new[k]
            fill_yz(step + 1, new, [times_i(x) for x in new], True)

    build(3, t_sign)
    loads[0].wait()
    v = [src[k] for k in range(12)]
    vi = [times_i(x) for x in v]
    for k in range(12):
        psi[k] = v[k]
    fill_t(0, v, vi, None)
    for mu in (1, 2, 0):
        build(mu, HOP)
    fill_yz(0, v, vi, False)
    def open_to(kind, way, answered):
        near = jnp.logical_not(far[way]) if kind == 0 else True
        side = calls[kind][way] if answered else hears[kind][way]

        @pl.when(jnp.logical_and(side, near) if answered else side)
        def _():
            if answered:
                pl.semaphore_wait(ok_sem.at[kind, way], 1)
            remote(0, kind, way).start()

    for kind in (0, 2, 1):
        for way in range(2):
            open_to(kind, way, False)

    @pl.when(early)
    def _():
        leave(0, onward).start()

    for kind, way in ((1, 0), (1, 1), (0, 0), (0, 1), (2, 1), (2, 0)):
        open_to(kind, way, True)

    loads[2].wait()
    loads[3].wait()
    for k in range(6):
        even, odd = spread(diag[k])
        c_dg[2 * k] = even
        c_dg[2 * k + 1] = odd
    for k in range(30):
        re, im = spread(off[k])
        c_re[k] = re
        c_im[k] = im

    step_body(0, True, False)

    hand_on(0)

    @pl.when(early)
    def _():
        pl.semaphore_wait(ok_sem.at[0, onward], 1)

    def loop_body(step, carry):
        step_body(step, False, False)
        return carry

    lax.fori_loop(1, ITERS - 1, loop_body, 0)
    step_body(ITERS - 1, False, True)

    @pl.when(jnp.logical_or(*holds))
    def _():
        pltpu.make_async_copy(park, park, park_send).wait()

    pltpu.make_async_copy(out, out, send_sem).wait()


def store(sol_ref, res_ref, sol_hbm, res_hbm, sem):
    copies = [
        pltpu.make_async_copy(sol_ref, sol_hbm, sem.at[0]),
        pltpu.make_async_copy(res_ref, res_hbm, sem.at[1]),
    ]
    for copy in copies:
        copy.start()
    for copy in copies:
        copy.wait()


def body(source, link_rows, clover_diag, clover_off):
    src = source.reshape(12, 8, 128)
    link = link_rows.reshape(24, 8, 128)
    diag = clover_diag.reshape(6, 8, 128)
    off = clover_off.reshape(30, 8, 128)
    field = pltpu.VMEM((12, 8, 128), F32)
    n_gy = lax.axis_size("gy")
    vmem = lambda *shape: pltpu.VMEM(shape + (8, 128), F32)
    solution, residual = pl.pallas_call(
        kernel,
        name="clover_steps",
        out_shape=(field, field),
        in_specs=[pl.BlockSpec(memory_space=pl.ANY)] * 4,
        out_specs=[pl.BlockSpec(memory_space=pltpu.VMEM)] * 2,
        scratch_shapes=[
            vmem(12), vmem(24), vmem(6), vmem(30),
            vmem(4, 9), vmem(4, 9), vmem(30), vmem(30), vmem(12), vmem(12), vmem(6), vmem(6),
            vmem(ITERS, 2, 10), vmem(ITERS, 2, 10), vmem(2, n_gy, 3),
            pltpu.SemaphoreType.DMA((4,)),
            pltpu.SemaphoreType.DMA,
            pltpu.SemaphoreType.DMA((ITERS, 2)),
            pltpu.SemaphoreType.DMA((2,)),
            pltpu.SemaphoreType.DMA((2,)),
            pltpu.SemaphoreType.REGULAR((3, 2)),
            pltpu.SemaphoreType.DMA((2, n_gy)),
            pltpu.SemaphoreType.REGULAR((n_gy,)),
            pltpu.SemaphoreType.DMA,
        ],
        compiler_params=pltpu.CompilerParams(collective_id=0, has_side_effects=True),
    )(src, link, diag, off)
    field = jax.ShapeDtypeStruct((12, 8, 128), F32)
    solution, residual = pl.pallas_call(
        store,
        name="store",
        out_shape=(field, field),
        in_specs=[pl.BlockSpec(memory_space=pltpu.VMEM)] * 2,
        out_specs=[pl.BlockSpec(memory_space=pl.ANY)] * 2,
        scratch_shapes=[pltpu.SemaphoreType.DMA((2,))],
    )(*(pltpu.with_memory_space_constraint(x, pltpu.VMEM) for x in (solution, residual)))
    return solution.reshape(source.shape), residual.reshape(source.shape)


def solution(mesh):
    in_specs = (
        P(None, None, None, "ta", "gz", "gy"),
        P(None, None, None, None, "ta", "gz", "gy"),
        P(None, None, "ta", "gz", "gy"),
        P(None, None, None, "ta", "gz", "gy"),
    )
    out_specs = (P(None, None, None, "ta", "gz", "gy"), P(None, None, None, "ta", "gz", "gy"))
    return jax.shard_map(body, mesh=mesh, in_specs=in_specs, out_specs=out_specs, check_vma=False)
```

```python
import jax
import jax.numpy as jnp
from jax import lax
from jax.experimental import pallas as pl
from jax.experimental.pallas import tpu as pltpu
from jax.sharding import PartitionSpec as P

NX = 32
ITERS = 4
HOP = 0.125
DAMP = 0.8
MESH = pl.DeviceIdType.MESH
AXES = ("ta", "gz", "gy")
GROUP = 4
F32 = jnp.float32


def lanes():
    return lax.broadcasted_iota(jnp.int32, (8, 128), 1)


def rows():
    return lax.broadcasted_iota(jnp.int32, (8, 128), 0)


def roll_rows(v, by):
    return pltpu.roll(v, by % 8, 0)


def roll_lanes(v, by):
    return pltpu.roll(v, by % 128, 1)


def kernel(
    src_hbm, link_hbm, diag_hbm, off_hbm, sol_ref, res_ref,
    src, link, diag, off, u_re, u_im, c_re, c_im, c_dg, psi, y_fwd, y_bwd,
    out, into, park, load_sem, send_sem, t_sem, z_sem, y_sem,
    ok_sem, park_in, park_ok, park_send,
):
    loads = [
        pltpu.make_async_copy(src_hbm, src, load_sem.at[0]),
        pltpu.make_async_copy(link_hbm, link, load_sem.at[1]),
        pltpu.make_async_copy(diag_hbm, diag, load_sem.at[2]),
        pltpu.make_async_copy(off_hbm, off, load_sem.at[3]),
    ]
    for load in loads:
        load.start()

    place = [lax.axis_index(a) for a in AXES]
    count = [lax.axis_size(a) for a in AXES]
    ahead = [jnp.where(p == n - 1, 0, p + 1) for p, n in zip(place, count)]
    back = [jnp.where(p == 0, n - 1, p - 1) for p, n in zip(place, count)]

    ta, gz, gy = place
    n_ta, n_gz, n_gy = count

    def upward(axis, p):
        if axis == 1:
            return jnp.logical_and(p % 2 == 1, p < n_gz - 1)
        return p < (n_ta - 2, None, n_gy - 1)[axis]

    hears = [(upward(a, back[a]), jnp.logical_not(upward(a, place[a]))) for a in range(3)]
    calls = [tuple(jnp.logical_not(h) for h in pair) for pair in hears]
    far = (lax.rem(ta, GROUP) == 0, lax.rem(ta, GROUP) == GROUP - 1)
    early = jnp.logical_or(ta == 0, ta == GROUP - 1)
    late = jnp.logical_or(ta == n_ta - 1, ta == GROUP)
    onward = jnp.logical_or(ta == GROUP - 1, ta == GROUP).astype(jnp.int32)
    holds = (jnp.logical_and(ta == GROUP - 1, gy == 0), jnp.logical_and(ta == 0, gy == n_gy - 1))
    holder_of = {
        "ta": jnp.where(onward == 1, 0, GROUP - 1), "gy": jnp.where(onward == 1, n_gy - 1, 0)
    }
    ends = ((0, n_ta - 1), (GROUP - 1, GROUP))

    def beside(axis, way):
        return {AXES[axis]: (back, ahead)[way][axis]}

    barrier = pltpu.get_barrier_semaphore()

    def call(axis, way):
        @pl.when(calls[axis][way])
        def _():
            pl.semaphore_signal(barrier, inc=1, device_id=beside(axis, way), device_id_type=MESH)

    for axis in range(3):
        for way in range(2):
            call(axis, way)

    for way in range(2):
        @pl.when(holds[way])
        def _(way=way):
            for g in range(n_gy):
                for t in ends[way]:
                    pl.semaphore_signal(barrier, inc=1, device_id={"ta": t, "gy": g}, device_id_type=MESH)

    expected = jnp.logical_or(early, late).astype(jnp.int32)
    for pair in hears:
        for h in pair:
            expected = expected + h.astype(jnp.int32)
    pl.semaphore_wait(barrier, expected)

    @pl.when(late)
    def _():
        pl.semaphore_signal(park_ok.at[gy], inc=1, device_id=holder_of, device_id_type=MESH)

    def answer(axis, way):
        @pl.when(hears[axis][way])
        def _():
            pl.semaphore_signal(
                ok_sem.at[axis, 1 - way], inc=1, device_id=beside(axis, way), device_id_type=MESH
            )

    for axis in range(3):
        for way in range(2):
            answer(axis, way)

    row, lane = rows(), lanes()
    upper = row < 4
    half = row % 2
    layer = (row // 2) % 2
    sign_j = jnp.where(upper, -1.0, 1.0).astype(F32)

    def times_i(v):
        return roll_rows(v, 4) * sign_j

    def spread(v):
        r = roll_rows(v, 4)
        return jnp.where(upper, v, r), jnp.where(upper, r, v)

    loads[1].wait()
    last = place[0] == count[0] - 1
    t_sign = jnp.where(jnp.logical_and(last, layer == 1), -HOP, HOP).astype(F32)
    conj = jnp.where(upper, 1.0, -1.0).astype(F32)

    def build(mu, weight):
        first = [link[6 * mu + c] for c in range(3)]
        second = [link[6 * mu + 3 + c] for c in range(3)]
        spread_first = [spread(v) for v in first]
        second_i = [times_i(v) for v in second]

        def product(a, b):
            return spread_first[a][0] * second[b] + spread_first[a][1] * second_i[b]

        for c in range(3):
            re, im = spread_first[c]
            u_re[mu, c] = re * weight
            u_im[mu, c] = im * weight
            re, im = spread(second[c])
            u_re[mu, 3 + c] = re * weight
            u_im[mu, 3 + c] = im * weight
            left, right = (c + 1) % 3, (c + 2) % 3
            third = (product(left, right) - product(right, left)) * conj
            re, im = spread(third)
            u_re[mu, 6 + c] = re * weight
            u_im[mu, 6 + c] = im * weight

    def remote(step, kind, way):
        part = pl.ds((0, 3, 9)[kind], (3, 6, 1)[kind])
        return pltpu.make_async_remote_copy(
            src_ref=out.at[step, way, part],
            dst_ref=into.at[step, way, part],
            send_sem=send_sem,
            recv_sem=(t_sem.at[step, way], z_sem.at[step % 2], y_sem.at[step % 2])[kind],
            device_id={AXES[kind]: (back, ahead)[way][kind]},
            device_id_type=MESH,
        )

    def wait_both(step, kind):
        part = into.at[step, :, pl.ds((0, 3, 9)[kind], (3, 6, 1)[kind])]
        pltpu.make_async_copy(part, part, (None, z_sem.at[step % 2], y_sem.at[step % 2])[kind]).wait()

    def multiply(mu, h, hi):
        out = []
        for spin in range(2):
            for i in range(3):
                total = None
                for j in range(3):
                    term = u_re[mu, 3 * i + j] * h[3 * spin + j] + u_im[mu, 3 * i + j] * hi[3 * spin + j]
                    total = term if total is None else total + term
                out.append(total)
        return out

    def multiply_adjoint(mu, h, hi):
        out = []
        for spin in range(2):
            for i in range(3):
                total = None
                for j in range(3):
                    term = u_re[mu, 3 * j + i] * h[3 * spin + j] - u_im[mu, 3 * j + i] * hi[3 * spin + j]
                    total = term if total is None else total + term
                out.append(total)
        return out

    def project(mu, factor, v, vi):
        def add(a, b, f):
            return a + b if f > 0 else a - b

        h, hi = [], []
        for c in range(3):
            p = [v[3 * s + c] for s in range(4)]
            q = [vi[3 * s + c] for s in range(4)]
            if mu == 0:
                h.append((add(p[0], q[3], factor), add(p[1], q[2], factor)))
                hi.append((add(q[0], p[3], -factor), add(q[1], p[2], -factor)))
            elif mu == 1:
                h.append((add(p[0], p[3], -factor), add(p[1], p[2], factor)))
                hi.append((add(q[0], q[3], -factor), add(q[1], q[2], factor)))
            elif mu == 2:
                h.append((add(p[0], q[2], factor), add(p[1], q[3], -factor)))
                hi.append((add(q[0], p[2], -factor), add(q[1], p[3], factor)))
            else:
                h.append((add(p[0], p[2], factor), add(p[1], p[3], factor)))
                hi.append((add(q[0], q[2], factor), add(q[1], q[3], factor)))
        flat = lambda pairs: [pairs[c][s] for s in range(2) for c in range(3)]
        return flat(h), flat(hi)

    def accumulate(mu, factor, h, acc, acc_i):
        def put(where, at, value, f):
            if where[at] is None:
                where[at] = value if f > 0 else -value
            else:
                where[at] = where[at] + value if f > 0 else where[at] - value

        for c in range(3):
            a, b = h[c], h[3 + c]
            put(acc, c, a, 1)
            put(acc, 3 + c, b, 1)
            if mu == 0:
                put(acc_i, c, b, -factor)
                put(acc_i, 3 + c, a, -factor)
            elif mu == 1:
                put(acc, 6 + c, b, factor)
                put(acc, 9 + c, a, -factor)
            elif mu == 2:
                put(acc_i, c, a, -factor)
                put(acc_i, 3 + c, b, factor)
            else:
                put(acc, 6 + c, a, factor)
                put(acc, 9 + c, b, factor)

    group = lane // 32
    x_place = lane % 32

    def pack_y(h):
        low = jnp.where(
            group < 2,
            jnp.where(group == 0, h[0], roll_lanes(h[1], 32)),
            jnp.where(group == 2, roll_lanes(h[2], 64), roll_lanes(h[3], 96)),
        )
        high = jnp.where(group == 0, h[4], roll_lanes(h[5], 32))
        return low, high

    def leave(step, way):
        return pltpu.make_async_remote_copy(
            src_ref=out.at[step, way, pl.ds(0, 3)],
            dst_ref=park.at[step, gy],
            send_sem=send_sem,
            recv_sem=park_in.at[step, gy],
            device_id=holder_of,
            device_id_type=MESH,
        )

    def hand_on(way):
        @pl.when(holds[way])
        def _():
            for step in range(2):
                for g in range(n_gy):
                    got = park.at[step, g]
                    pltpu.make_async_copy(got, got, park_in.at[step, g]).wait()
                    if step == 0:
                        pl.semaphore_wait(park_ok.at[g], 1)
                    pltpu.make_async_remote_copy(
                        src_ref=got,
                        dst_ref=into.at[step, way, pl.ds(0, 3)],
                        send_sem=park_send,
                        recv_sem=t_sem.at[step, way],
                        device_id={"ta": ends[way][1], "gy": g},
                        device_id_type=MESH,
                    ).start()

    def fill_t(step, v, vi, send):
        h, _ = project(3, -1, v, vi)
        for k in range(3):
            out[step, 0, k] = jnp.where(layer == 0, h[k], roll_rows(h[3 + k], 2))
        if send:
            send(step, 0)
        h, hi = project(3, 1, v, vi)
        h = multiply_adjoint(3, h, hi)
        for k in range(3):
            out[step, 1, k] = jnp.where(layer == 1, h[k], roll_rows(h[3 + k], -2))
        if send:
            send(step, 1)

    def send_t(step, way):
        remote(step, 0, way).start()

    def send_or_leave(step, way):
        mine = jnp.logical_and(early, onward == way)

        @pl.when(jnp.logical_not(mine))
        def _():
            remote(step, 0, way).start()

        @pl.when(mine)
        def _():
            leave(step, way).start()

    def fill_yz(step, v, vi, send):
        h, _ = project(1, -1, v, vi)
        low, high = pack_y(h)
        out[step, 0, 9] = jnp.where(half == 0, low, roll_rows(high, 1))
        if send:
            remote(step, 2, 0).start()
        for k in range(6):
            y_fwd[k] = h[k]
        h, hi = project(1, 1, v, vi)
        h = multiply_adjoint(1, h, hi)
        h = [roll_lanes(x, 32) for x in h]
        low, high = pack_y(h)
        out[step, 1, 9] = jnp.where(half == 1, low, roll_rows(high, -1))
        if send:
            remote(step, 2, 1).start()
        for k in range(6):
            y_bwd[k] = h[k]
        h, _ = project(2, -1, v, vi)
        for k in range(6):
            out[step, 0, 3 + k] = h[k]
        if send:
            remote(step, 1, 0).start()
        h, hi = project(2, 1, v, vi)
        h = multiply_adjoint(2, h, hi)
        for k in range(6):
            out[step, 1, 3 + k] = h[k]
        if send:
            remote(step, 1, 1).start()

    def step_body(step, begin, final):
        v = [psi[k] for k in range(12)]
        vi = [times_i(x) for x in v]

        acc = [None] * 12
        acc_i = [None] * 6
        h, _ = project(0, -1, v, vi)
        h = [jnp.where(x_place == 31, roll_lanes(x, 31), roll_lanes(x, -1)) for x in h]
        accumulate(0, -1, multiply(0, h, [times_i(x) for x in h]), acc, acc_i)
        h, hi = project(0, 1, v, vi)
        h = multiply_adjoint(0, h, hi)
        h = [jnp.where(x_place == 0, roll_lanes(x, -31), roll_lanes(x, 1)) for x in h]
        accumulate(0, 1, h, acc, acc_i)
        h, _ = project(3, -1, v, vi)
        h = [jnp.where(layer == 0, roll_rows(x, -2), 0.0) for x in h]
        accumulate(3, -1, multiply(3, h, [times_i(x) for x in h]), acc, acc_i)
        h, hi = project(3, 1, v, vi)
        h = multiply_adjoint(3, h, hi)
        h = [jnp.where(layer == 1, roll_rows(x, 2), 0.0) for x in h]
        accumulate(3, 1, h, acc, acc_i)

        for b in range(2):
            image = [c_dg[6 * b + i] * v[6 * b + i] for i in range(6)]
            pair = 15 * b
            for i in range(6):
                for j in range(i + 1, 6):
                    re, im = c_re[pair], c_im[pair]
                    image[i] = image[i] + (re * v[6 * b + j] + im * vi[6 * b + j])
                    image[j] = image[j] + (re * v[6 * b + i] - im * vi[6 * b + i])
                    pair += 1
            for i in range(6):
                k = 6 * b + i
                acc[k] = acc[k] + (src[k] - image[i])

        wait_both(step, 1)
        h = [into[step, 0, 3 + k] for k in range(6)]
        accumulate(2, -1, multiply(2, h, [times_i(x) for x in h]), acc, acc_i)
        accumulate(2, 1, [into[step, 1, 3 + k] for k in range(6)], acc, acc_i)
        for k in range(6):
            acc[6 + k] = acc[6 + k] + times_i(acc_i[k])

        wait_both(step, 2)
        got = into[step, 0, 9]
        moved = roll_rows(got, 1)
        halo = [
            roll_lanes(moved, 96), roll_lanes(moved, 64), roll_lanes(moved, 32), moved,
            roll_lanes(got, 96), roll_lanes(got, 64),
        ]
        h = []
        for k in range(6):
            r = roll_lanes(y_fwd[k], -32)
            edge = jnp.where(half == 0, roll_rows(r, -1), halo[k])
            h.append(jnp.where(group == 3, edge, r))
        accumulate(1, -1, multiply(1, h, [times_i(x) for x in h]), acc, acc_i)
        got = into[step, 1, 9]
        moved = roll_rows(got, -1)
        halo = [
            moved, roll_lanes(moved, 96), roll_lanes(moved, 64), roll_lanes(moved, 32),
            got, roll_lanes(got, 96),
        ]
        h = []
        for k in range(6):
            r = y_bwd[k]
            edge = jnp.where(half == 1, roll_rows(r, 1), halo[k])
            h.append(jnp.where(group == 0, edge, r))
        accumulate(1, 1, h, acc, acc_i)

        if begin:
            @pl.when(jnp.logical_and(jnp.logical_and(far[1], calls[0][1]), jnp.logical_not(early)))
            def _():
                pl.semaphore_wait(ok_sem.at[0, 1], 1)
                remote(0, 0, 1).start()

        if not final:
            part = [v[k] + DAMP * acc[k] for k in range(12)]
            fill_t(step + 1, part, [times_i(x) for x in part], send_or_leave if begin else send_t)
        if begin:
            hand_on(1)

        remote(step, 0, 0).wait_recv()
        h = []
        for k in range(6):
            got = into[step, 0, k % 3]
            halo = roll_rows(got, 2) if k < 3 else got
            h.append(jnp.where(layer == 0, 0.0, halo))
        accumulate(3, -1, multiply(3, h, [times_i(x) for x in h]), acc, acc_i)
        remote(step, 0, 1).wait_recv()
        h = []
        for k in range(6):
            got = into[step, 1, k % 3]
            halo = roll_rows(got, -2) if k < 3 else got
            h.append(jnp.where(layer == 1, 0.0, halo))
        accumulate(3, 1, h, acc, acc_i)

        new = [v[k] + DAMP * acc[k] for k in range(12)]
        if final:
            for k in range(12):
                res_ref[k] = acc[k]
                sol_ref[k] = new[k]
        else:
            for k in range(12):
                psi[k] = new[k]
            fill_yz(step + 1, new, [times_i(x) for x in new], True)

    build(3, t_sign)
    loads[0].wait()
    v = [src[k] for k in range(12)]
    vi = [times_i(x) for x in v]
    for k in range(12):
        psi[k] = v[k]
    fill_t(0, v, vi, None)
    for mu in (1, 2, 0):
        build(mu, HOP)
    fill_yz(0, v, vi, False)
    def open_to(kind, way, answered):
        near = jnp.logical_not(far[way]) if kind == 0 else True
        side = calls[kind][way] if answered else hears[kind][way]

        @pl.when(jnp.logical_and(side, near) if answered else side)
        def _():
            if answered:
                pl.semaphore_wait(ok_sem.at[kind, way], 1)
            remote(0, kind, way).start()

    for kind in (0, 2, 1):
        for way in range(2):
            open_to(kind, way, False)

    @pl.when(early)
    def _():
        leave(0, onward).start()

    for kind, way in ((1, 0), (1, 1), (0, 0), (0, 1), (2, 1), (2, 0)):
        open_to(kind, way, True)

    loads[2].wait()
    loads[3].wait()
    for k in range(6):
        even, odd = spread(diag[k])
        c_dg[2 * k] = even
        c_dg[2 * k + 1] = odd
    for k in range(30):
        re, im = spread(off[k])
        c_re[k] = re
        c_im[k] = im

    step_body(0, True, False)

    hand_on(0)

    @pl.when(early)
    def _():
        pl.semaphore_wait(ok_sem.at[0, onward], 1)

    for step in range(1, ITERS - 1):
        step_body(step, False, False)
    step_body(ITERS - 1, False, True)

    @pl.when(jnp.logical_or(*holds))
    def _():
        pltpu.make_async_copy(park, park, park_send).wait()

    pltpu.make_async_copy(out, out, send_sem).wait()


def store(sol_ref, res_ref, sol_hbm, res_hbm, sem):
    copies = [
        pltpu.make_async_copy(sol_ref, sol_hbm, sem.at[0]),
        pltpu.make_async_copy(res_ref, res_hbm, sem.at[1]),
    ]
    for copy in copies:
        copy.start()
    for copy in copies:
        copy.wait()


def body(source, link_rows, clover_diag, clover_off):
    src = source.reshape(12, 8, 128)
    link = link_rows.reshape(24, 8, 128)
    diag = clover_diag.reshape(6, 8, 128)
    off = clover_off.reshape(30, 8, 128)
    field = pltpu.VMEM((12, 8, 128), F32)
    n_gy = lax.axis_size("gy")
    vmem = lambda *shape: pltpu.VMEM(shape + (8, 128), F32)
    solution, residual = pl.pallas_call(
        kernel,
        name="clover_steps",
        out_shape=(field, field),
        in_specs=[pl.BlockSpec(memory_space=pl.ANY)] * 4,
        out_specs=[pl.BlockSpec(memory_space=pltpu.VMEM)] * 2,
        scratch_shapes=[
            vmem(12), vmem(24), vmem(6), vmem(30),
            vmem(4, 9), vmem(4, 9), vmem(30), vmem(30), vmem(12), vmem(12), vmem(6), vmem(6),
            vmem(ITERS, 2, 10), vmem(ITERS, 2, 10), vmem(2, n_gy, 3),
            pltpu.SemaphoreType.DMA((4,)),
            pltpu.SemaphoreType.DMA,
            pltpu.SemaphoreType.DMA((ITERS, 2)),
            pltpu.SemaphoreType.DMA((2,)),
            pltpu.SemaphoreType.DMA((2,)),
            pltpu.SemaphoreType.REGULAR((3, 2)),
            pltpu.SemaphoreType.DMA((2, n_gy)),
            pltpu.SemaphoreType.REGULAR((n_gy,)),
            pltpu.SemaphoreType.DMA,
        ],
        compiler_params=pltpu.CompilerParams(collective_id=0, has_side_effects=True),
    )(src, link, diag, off)
    field = jax.ShapeDtypeStruct((12, 8, 128), F32)
    solution, residual = pl.pallas_call(
        store,
        name="store",
        out_shape=(field, field),
        in_specs=[pl.BlockSpec(memory_space=pltpu.VMEM)] * 2,
        out_specs=[pl.BlockSpec(memory_space=pl.ANY)] * 2,
        scratch_shapes=[pltpu.SemaphoreType.DMA((2,))],
    )(*(pltpu.with_memory_space_constraint(x, pltpu.VMEM) for x in (solution, residual)))
    return solution.reshape(source.shape), residual.reshape(source.shape)


def solution(mesh):
    in_specs = (
        P(None, None, None, "ta", "gz", "gy"),
        P(None, None, None, None, "ta", "gz", "gy"),
        P(None, None, "ta", "gz", "gy"),
        P(None, None, None, "ta", "gz", "gy"),
    )
    out_specs = (P(None, None, None, "ta", "gz", "gy"), P(None, None, None, "ta", "gz", "gy"))
    return jax.shard_map(body, mesh=mesh, in_specs=in_specs, out_specs=out_specs, check_vma=False)
```

```python
import jax
import jax.numpy as jnp
from jax import lax
from jax.experimental import pallas as pl
from jax.experimental.pallas import tpu as pltpu
from jax.sharding import PartitionSpec as P

NX = 32
ITERS = 4
HOP = 0.125
DAMP = 0.8
MESH = pl.DeviceIdType.MESH
AXES = ("ta", "gz", "gy")
GROUP = 4
F32 = jnp.float32


def lanes():
    return lax.broadcasted_iota(jnp.int32, (8, 128), 1)


def rows():
    return lax.broadcasted_iota(jnp.int32, (8, 128), 0)


def roll_rows(v, by):
    return pltpu.roll(v, by % 8, 0)


def roll_lanes(v, by):
    return pltpu.roll(v, by % 128, 1)


def kernel(
    src_hbm, link_hbm, diag_hbm, off_hbm, sol_ref, res_ref,
    src, link, diag, off, u_re, u_im, c_re, c_im, c_dg, psi, y_fwd, y_bwd,
    out, into, park, load_sem, send_sem, t_sem, z_sem, y_sem,
    ok_sem, park_in, park_ok, park_send,
):
    loads = [
        pltpu.make_async_copy(src_hbm, src, load_sem.at[0]),
        pltpu.make_async_copy(link_hbm, link, load_sem.at[1]),
        pltpu.make_async_copy(diag_hbm, diag, load_sem.at[2]),
        pltpu.make_async_copy(off_hbm, off, load_sem.at[3]),
    ]
    for load in loads:
        load.start()

    place = [lax.axis_index(a) for a in AXES]
    count = [lax.axis_size(a) for a in AXES]
    ahead = [jnp.where(p == n - 1, 0, p + 1) for p, n in zip(place, count)]
    back = [jnp.where(p == 0, n - 1, p - 1) for p, n in zip(place, count)]

    ta, gz, gy = place
    n_ta, n_gz, n_gy = count

    def upward(axis, p):
        if axis == 1:
            return jnp.logical_and(p % 2 == 1, p < n_gz - 1)
        return p < (n_ta - 2, None, n_gy - 1)[axis]

    hears = [(upward(a, back[a]), jnp.logical_not(upward(a, place[a]))) for a in range(3)]
    calls = [tuple(jnp.logical_not(h) for h in pair) for pair in hears]
    far = (lax.rem(ta, GROUP) == 0, lax.rem(ta, GROUP) == GROUP - 1)
    early = jnp.logical_or(ta == 0, ta == GROUP - 1)
    late = jnp.logical_or(ta == n_ta - 1, ta == GROUP)
    onward = jnp.logical_or(ta == GROUP - 1, ta == GROUP).astype(jnp.int32)
    holds = (jnp.logical_and(ta == GROUP - 1, gy == 0), jnp.logical_and(ta == 0, gy == n_gy - 1))
    holder_of = {
        "ta": jnp.where(onward == 1, 0, GROUP - 1), "gy": jnp.where(onward == 1, n_gy - 1, 0)
    }
    ends = ((0, n_ta - 1), (GROUP - 1, GROUP))

    def beside(axis, way):
        return {AXES[axis]: (back, ahead)[way][axis]}

    barrier = pltpu.get_barrier_semaphore()

    def call(axis, way):
        @pl.when(calls[axis][way])
        def _():
            pl.semaphore_signal(barrier, inc=1, device_id=beside(axis, way), device_id_type=MESH)

    for axis in (2, 0, 1):
        for way in range(2):
            call(axis, way)

    for way in range(2):
        @pl.when(holds[way])
        def _(way=way):
            for g in range(n_gy):
                for t in ends[way]:
                    pl.semaphore_signal(barrier, inc=1, device_id={"ta": t, "gy": g}, device_id_type=MESH)

    expected = jnp.logical_or(early, late).astype(jnp.int32)
    for pair in hears:
        for h in pair:
            expected = expected + h.astype(jnp.int32)
    pl.semaphore_wait(barrier, expected)

    @pl.when(late)
    def _():
        pl.semaphore_signal(park_ok.at[gy], inc=1, device_id=holder_of, device_id_type=MESH)

    def answer(axis, way):
        @pl.when(hears[axis][way])
        def _():
            pl.semaphore_signal(
                ok_sem.at[axis, 1 - way], inc=1, device_id=beside(axis, way), device_id_type=MESH
            )

    for axis in (2, 0, 1):
        for way in range(2):
            answer(axis, way)

    row, lane = rows(), lanes()
    upper = row < 4
    half = row % 2
    layer = (row // 2) % 2
    sign_j = jnp.where(upper, -1.0, 1.0).astype(F32)

    def times_i(v):
        return roll_rows(v, 4) * sign_j

    def spread(v):
        r = roll_rows(v, 4)
        return jnp.where(upper, v, r), jnp.where(upper, r, v)

    loads[1].wait()
    last = place[0] == count[0] - 1
    t_sign = jnp.where(jnp.logical_and(last, layer == 1), -HOP, HOP).astype(F32)
    conj = jnp.where(upper, 1.0, -1.0).astype(F32)

    def build(mu, weight):
        first = [link[6 * mu + c] for c in range(3)]
        second = [link[6 * mu + 3 + c] for c in range(3)]
        spread_first = [spread(v) for v in first]
        second_i = [times_i(v) for v in second]

        def product(a, b):
            return spread_first[a][0] * second[b] + spread_first[a][1] * second_i[b]

        for c in range(3):
            re, im = spread_first[c]
            u_re[mu, c] = re * weight
            u_im[mu, c] = im * weight
            re, im = spread(second[c])
            u_re[mu, 3 + c] = re * weight
            u_im[mu, 3 + c] = im * weight
            left, right = (c + 1) % 3, (c + 2) % 3
            third = (product(left, right) - product(right, left)) * conj
            re, im = spread(third)
            u_re[mu, 6 + c] = re * weight
            u_im[mu, 6 + c] = im * weight

    def remote(step, kind, way):
        part = pl.ds((0, 3, 9)[kind], (3, 6, 1)[kind])
        return pltpu.make_async_remote_copy(
            src_ref=out.at[step, way, part],
            dst_ref=into.at[step, way, part],
            send_sem=send_sem,
            recv_sem=(t_sem.at[step, way], z_sem.at[step % 2], y_sem.at[step % 2])[kind],
            device_id={AXES[kind]: (back, ahead)[way][kind]},
            device_id_type=MESH,
        )

    def wait_both(step, kind):
        part = into.at[step, :, pl.ds((0, 3, 9)[kind], (3, 6, 1)[kind])]
        pltpu.make_async_copy(part, part, (None, z_sem.at[step % 2], y_sem.at[step % 2])[kind]).wait()

    def multiply(mu, h, hi):
        out = []
        for spin in range(2):
            for i in range(3):
                total = None
                for j in range(3):
                    term = u_re[mu, 3 * i + j] * h[3 * spin + j] + u_im[mu, 3 * i + j] * hi[3 * spin + j]
                    total = term if total is None else total + term
                out.append(total)
        return out

    def multiply_adjoint(mu, h, hi):
        out = []
        for spin in range(2):
            for i in range(3):
                total = None
                for j in range(3):
                    term = u_re[mu, 3 * j + i] * h[3 * spin + j] - u_im[mu, 3 * j + i] * hi[3 * spin + j]
                    total = term if total is None else total + term
                out.append(total)
        return out

    def project(mu, factor, v, vi):
        def add(a, b, f):
            return a + b if f > 0 else a - b

        h, hi = [], []
        for c in range(3):
            p = [v[3 * s + c] for s in range(4)]
            q = [vi[3 * s + c] for s in range(4)]
            if mu == 0:
                h.append((add(p[0], q[3], factor), add(p[1], q[2], factor)))
                hi.append((add(q[0], p[3], -factor), add(q[1], p[2], -factor)))
            elif mu == 1:
                h.append((add(p[0], p[3], -factor), add(p[1], p[2], factor)))
                hi.append((add(q[0], q[3], -factor), add(q[1], q[2], factor)))
            elif mu == 2:
                h.append((add(p[0], q[2], factor), add(p[1], q[3], -factor)))
                hi.append((add(q[0], p[2], -factor), add(q[1], p[3], factor)))
            else:
                h.append((add(p[0], p[2], factor), add(p[1], p[3], factor)))
                hi.append((add(q[0], q[2], factor), add(q[1], q[3], factor)))
        flat = lambda pairs: [pairs[c][s] for s in range(2) for c in range(3)]
        return flat(h), flat(hi)

    def accumulate(mu, factor, h, acc, acc_i):
        def put(where, at, value, f):
            if where[at] is None:
                where[at] = value if f > 0 else -value
            else:
                where[at] = where[at] + value if f > 0 else where[at] - value

        for c in range(3):
            a, b = h[c], h[3 + c]
            put(acc, c, a, 1)
            put(acc, 3 + c, b, 1)
            if mu == 0:
                put(acc_i, c, b, -factor)
                put(acc_i, 3 + c, a, -factor)
            elif mu == 1:
                put(acc, 6 + c, b, factor)
                put(acc, 9 + c, a, -factor)
            elif mu == 2:
                put(acc_i, c, a, -factor)
                put(acc_i, 3 + c, b, factor)
            else:
                put(acc, 6 + c, a, factor)
                put(acc, 9 + c, b, factor)

    group = lane // 32
    x_place = lane % 32

    def pack_y(h):
        low = jnp.where(
            group < 2,
            jnp.where(group == 0, h[0], roll_lanes(h[1], 32)),
            jnp.where(group == 2, roll_lanes(h[2], 64), roll_lanes(h[3], 96)),
        )
        high = jnp.where(group == 0, h[4], roll_lanes(h[5], 32))
        return low, high

    def leave(step, way):
        return pltpu.make_async_remote_copy(
            src_ref=out.at[step, way, pl.ds(0, 3)],
            dst_ref=park.at[step, gy],
            send_sem=send_sem,
            recv_sem=park_in.at[step, gy],
            device_id=holder_of,
            device_id_type=MESH,
        )

    def hand_on(way):
        @pl.when(holds[way])
        def _():
            for step in range(2):
                for g in range(n_gy):
                    got = park.at[step, g]
                    pltpu.make_async_copy(got, got, park_in.at[step, g]).wait()
                    if step == 0:
                        pl.semaphore_wait(park_ok.at[g], 1)
                    pltpu.make_async_remote_copy(
                        src_ref=got,
                        dst_ref=into.at[step, way, pl.ds(0, 3)],
                        send_sem=park_send,
                        recv_sem=t_sem.at[step, way],
                        device_id={"ta": ends[way][1], "gy": g},
                        device_id_type=MESH,
                    ).start()

    def fill_t(step, v, vi, send):
        h, _ = project(3, -1, v, vi)
        for k in range(3):
            out[step, 0, k] = jnp.where(layer == 0, h[k], roll_rows(h[3 + k], 2))
        if send:
            send(step, 0)
        h, hi = project(3, 1, v, vi)
        h = multiply_adjoint(3, h, hi)
        for k in range(3):
            out[step, 1, k] = jnp.where(layer == 1, h[k], roll_rows(h[3 + k], -2))
        if send:
            send(step, 1)

    def send_t(step, way):
        remote(step, 0, way).start()

    def send_or_leave(step, way):
        mine = jnp.logical_and(early, onward == way)

        @pl.when(jnp.logical_not(mine))
        def _():
            remote(step, 0, way).start()

        @pl.when(mine)
        def _():
            leave(step, way).start()

    def fill_yz(step, v, vi, send):
        h, _ = project(1, -1, v, vi)
        low, high = pack_y(h)
        out[step, 0, 9] = jnp.where(half == 0, low, roll_rows(high, 1))
        if send:
            remote(step, 2, 0).start()
        for k in range(6):
            y_fwd[k] = h[k]
        h, hi = project(1, 1, v, vi)
        h = multiply_adjoint(1, h, hi)
        h = [roll_lanes(x, 32) for x in h]
        low, high = pack_y(h)
        out[step, 1, 9] = jnp.where(half == 1, low, roll_rows(high, -1))
        if send:
            remote(step, 2, 1).start()
        for k in range(6):
            y_bwd[k] = h[k]
        h, _ = project(2, -1, v, vi)
        for k in range(6):
            out[step, 0, 3 + k] = h[k]
        if send:
            remote(step, 1, 0).start()
        h, hi = project(2, 1, v, vi)
        h = multiply_adjoint(2, h, hi)
        for k in range(6):
            out[step, 1, 3 + k] = h[k]
        if send:
            remote(step, 1, 1).start()

    def step_body(step, begin, final):
        v = [psi[k] for k in range(12)]
        vi = [times_i(x) for x in v]

        acc = [None] * 12
        acc_i = [None] * 6
        h, _ = project(0, -1, v, vi)
        h = [jnp.where(x_place == 31, roll_lanes(x, 31), roll_lanes(x, -1)) for x in h]
        accumulate(0, -1, multiply(0, h, [times_i(x) for x in h]), acc, acc_i)
        h, hi = project(0, 1, v, vi)
        h = multiply_adjoint(0, h, hi)
        h = [jnp.where(x_place == 0, roll_lanes(x, -31), roll_lanes(x, 1)) for x in h]
        accumulate(0, 1, h, acc, acc_i)
        h, _ = project(3, -1, v, vi)
        h = [jnp.where(layer == 0, roll_rows(x, -2), 0.0) for x in h]
        accumulate(3, -1, multiply(3, h, [times_i(x) for x in h]), acc, acc_i)
        h, hi = project(3, 1, v, vi)
        h = multiply_adjoint(3, h, hi)
        h = [jnp.where(layer == 1, roll_rows(x, 2), 0.0) for x in h]
        accumulate(3, 1, h, acc, acc_i)

        for b in range(2):
            image = [c_dg[6 * b + i] * v[6 * b + i] for i in range(6)]
            pair = 15 * b
            for i in range(6):
                for j in range(i + 1, 6):
                    re, im = c_re[pair], c_im[pair]
                    image[i] = image[i] + (re * v[6 * b + j] + im * vi[6 * b + j])
                    image[j] = image[j] + (re * v[6 * b + i] - im * vi[6 * b + i])
                    pair += 1
            for i in range(6):
                k = 6 * b + i
                acc[k] = acc[k] + (src[k] - image[i])

        wait_both(step, 1)
        h = [into[step, 0, 3 + k] for k in range(6)]
        accumulate(2, -1, multiply(2, h, [times_i(x) for x in h]), acc, acc_i)
        accumulate(2, 1, [into[step, 1, 3 + k] for k in range(6)], acc, acc_i)
        for k in range(6):
            acc[6 + k] = acc[6 + k] + times_i(acc_i[k])

        wait_both(step, 2)
        got = into[step, 0, 9]
        moved = roll_rows(got, 1)
        halo = [
            roll_lanes(moved, 96), roll_lanes(moved, 64), roll_lanes(moved, 32), moved,
            roll_lanes(got, 96), roll_lanes(got, 64),
        ]
        h = []
        for k in range(6):
            r = roll_lanes(y_fwd[k], -32)
            edge = jnp.where(half == 0, roll_rows(r, -1), halo[k])
            h.append(jnp.where(group == 3, edge, r))
        accumulate(1, -1, multiply(1, h, [times_i(x) for x in h]), acc, acc_i)
        got = into[step, 1, 9]
        moved = roll_rows(got, -1)
        halo = [
            moved, roll_lanes(moved, 96), roll_lanes(moved, 64), roll_lanes(moved, 32),
            got, roll_lanes(got, 96),
        ]
        h = []
        for k in range(6):
            r = y_bwd[k]
            edge = jnp.where(half == 1, roll_rows(r, 1), halo[k])
            h.append(jnp.where(group == 0, edge, r))
        accumulate(1, 1, h, acc, acc_i)

        if begin:
            @pl.when(jnp.logical_and(jnp.logical_and(far[1], calls[0][1]), jnp.logical_not(early)))
            def _():
                pl.semaphore_wait(ok_sem.at[0, 1], 1)
                remote(0, 0, 1).start()

        if not final:
            part = [v[k] + DAMP * acc[k] for k in range(12)]
            fill_t(step + 1, part, [times_i(x) for x in part], send_or_leave if begin else send_t)
        if begin:
            hand_on(1)

        remote(step, 0, 0).wait_recv()
        h = []
        for k in range(6):
            got = into[step, 0, k % 3]
            halo = roll_rows(got, 2) if k < 3 else got
            h.append(jnp.where(layer == 0, 0.0, halo))
        accumulate(3, -1, multiply(3, h, [times_i(x) for x in h]), acc, acc_i)
        remote(step, 0, 1).wait_recv()
        h = []
        for k in range(6):
            got = into[step, 1, k % 3]
            halo = roll_rows(got, -2) if k < 3 else got
            h.append(jnp.where(layer == 1, 0.0, halo))
        accumulate(3, 1, h, acc, acc_i)

        new = [v[k] + DAMP * acc[k] for k in range(12)]
        if final:
            for k in range(12):
                res_ref[k] = acc[k]
                sol_ref[k] = new[k]
        else:
            for k in range(12):
                psi[k] = new[k]
            fill_yz(step + 1, new, [times_i(x) for x in new], True)

    build(3, t_sign)
    loads[0].wait()
    v = [src[k] for k in range(12)]
    vi = [times_i(x) for x in v]
    for k in range(12):
        psi[k] = v[k]
    fill_t(0, v, vi, None)
    for mu in (1, 2, 0):
        build(mu, HOP)
    fill_yz(0, v, vi, False)
    def open_to(kind, way, answered):
        near = jnp.logical_not(far[way]) if kind == 0 else True
        side = calls[kind][way] if answered else hears[kind][way]

        @pl.when(jnp.logical_and(side, near) if answered else side)
        def _():
            if answered:
                pl.semaphore_wait(ok_sem.at[kind, way], 1)
            remote(0, kind, way).start()

    for kind in (0, 2, 1):
        for way in range(2):
            open_to(kind, way, False)

    @pl.when(early)
    def _():
        leave(0, onward).start()

    for kind, way in ((1, 0), (1, 1), (0, 0), (0, 1), (2, 1), (2, 0)):
        open_to(kind, way, True)

    loads[2].wait()
    loads[3].wait()
    for k in range(6):
        even, odd = spread(diag[k])
        c_dg[2 * k] = even
        c_dg[2 * k + 1] = odd
    for k in range(30):
        re, im = spread(off[k])
        c_re[k] = re
        c_im[k] = im

    step_body(0, True, False)

    hand_on(0)

    @pl.when(early)
    def _():
        pl.semaphore_wait(ok_sem.at[0, onward], 1)

    for step in range(1, ITERS - 1):
        step_body(step, False, False)
    step_body(ITERS - 1, False, True)

    @pl.when(jnp.logical_or(*holds))
    def _():
        pltpu.make_async_copy(park, park, park_send).wait()

    pltpu.make_async_copy(out, out, send_sem).wait()


def store(sol_ref, res_ref, sol_hbm, res_hbm, sem):
    copies = [
        pltpu.make_async_copy(sol_ref, sol_hbm, sem.at[0]),
        pltpu.make_async_copy(res_ref, res_hbm, sem.at[1]),
    ]
    for copy in copies:
        copy.start()
    for copy in copies:
        copy.wait()


def body(source, link_rows, clover_diag, clover_off):
    src = source.reshape(12, 8, 128)
    link = link_rows.reshape(24, 8, 128)
    diag = clover_diag.reshape(6, 8, 128)
    off = clover_off.reshape(30, 8, 128)
    field = pltpu.VMEM((12, 8, 128), F32)
    n_gy = lax.axis_size("gy")
    vmem = lambda *shape: pltpu.VMEM(shape + (8, 128), F32)
    solution, residual = pl.pallas_call(
        kernel,
        name="clover_steps",
        out_shape=(field, field),
        in_specs=[pl.BlockSpec(memory_space=pl.ANY)] * 4,
        out_specs=[pl.BlockSpec(memory_space=pltpu.VMEM)] * 2,
        scratch_shapes=[
            vmem(12), vmem(24), vmem(6), vmem(30),
            vmem(4, 9), vmem(4, 9), vmem(30), vmem(30), vmem(12), vmem(12), vmem(6), vmem(6),
            vmem(ITERS, 2, 10), vmem(ITERS, 2, 10), vmem(2, n_gy, 3),
            pltpu.SemaphoreType.DMA((4,)),
            pltpu.SemaphoreType.DMA,
            pltpu.SemaphoreType.DMA((ITERS, 2)),
            pltpu.SemaphoreType.DMA((2,)),
            pltpu.SemaphoreType.DMA((2,)),
            pltpu.SemaphoreType.REGULAR((3, 2)),
            pltpu.SemaphoreType.DMA((2, n_gy)),
            pltpu.SemaphoreType.REGULAR((n_gy,)),
            pltpu.SemaphoreType.DMA,
        ],
        compiler_params=pltpu.CompilerParams(collective_id=0, has_side_effects=True),
    )(src, link, diag, off)
    field = jax.ShapeDtypeStruct((12, 8, 128), F32)
    solution, residual = pl.pallas_call(
        store,
        name="store",
        out_shape=(field, field),
        in_specs=[pl.BlockSpec(memory_space=pltpu.VMEM)] * 2,
        out_specs=[pl.BlockSpec(memory_space=pl.ANY)] * 2,
        scratch_shapes=[pltpu.SemaphoreType.DMA((2,))],
    )(*(pltpu.with_memory_space_constraint(x, pltpu.VMEM) for x in (solution, residual)))
    return solution.reshape(source.shape), residual.reshape(source.shape)


def solution(mesh):
    in_specs = (
        P(None, None, None, "ta", "gz", "gy"),
        P(None, None, None, None, "ta", "gz", "gy"),
        P(None, None, "ta", "gz", "gy"),
        P(None, None, None, "ta", "gz", "gy"),
    )
    out_specs = (P(None, None, None, "ta", "gz", "gy"), P(None, None, None, "ta", "gz", "gy"))
    return jax.shard_map(body, mesh=mesh, in_specs=in_specs, out_specs=out_specs, check_vma=False)
```
